512 devices in a mesh: dp: 4 (over z_lo), row: 8 (over y, core), col: 16 (over z_hi, x).
Axes of the slice: x: 4, y: 4, z: 16 (z_hi: 4, z_lo: 4; z = z_hi * 4 + z_lo), core: 2. Of those that a mesh axis runs over, the one named last changes fastest.
Arguments:
- queries: bfloat16 [4, 64, 256, 768], P('dp', 'row', 'col'), may hold values from -5.5 to 5.5
- keys: bfloat16 [4, 64, 256, 768], P('dp', 'row', 'col'), may hold values from -5.5 to 5.5
- values: bfloat16 [4, 64, 256, 768], P('dp', 'row', 'col'), may hold values from -6 to 6
- occupancy: int32 [4, 8, 32], P('dp', 'row', 'col'), may hold values from 0 to 64, as said below
- out_weight: bfloat16 [768, 768], P('dp'), may hold values from -0.21875 to 0.21875
- grad_out: bfloat16 [4, 64, 256, 768], P('dp', 'row', 'col'), may hold values from -6 to 6
Outputs:
- grad_queries: bfloat16 [4, 64, 256, 768], P('dp', 'row', 'col')
- grad_keys: bfloat16 [4, 64, 256, 768], P('dp', 'row', 'col')
- grad_values: bfloat16 [4, 64, 256, 768], P('dp', 'row', 'col')
- grad_weight: float32 [768, 768], P('dp')
The draws below stay inside these ranges and needn't reach their ends.
Inputs may be any that keep to these rules, and one draw needn't show every extreme that they name: `occupancy`: the occupied tiles of a block are its first that many tiles, row by row over its 8 x 8 tiles. Every slide has a block holding 8 * 8 and a block holding 0.
All inputs are finite; a program needn't handle non-finite values.
Results may differ from the reference program's by a relative error of at most 0.02.
Values may be sent and summed in bfloat16 or wider, within the bound.
A program may use at most 64 MiB of HBM per device.

```python
import jax
import jax.numpy as jnp
from jax import lax

HEADS = 12
HEAD_DIM = 64
OUT = 768
SIDE = 8
REACH = 3
CH = 768
SLIDES = 4
ROWS = 64
COLS = 256
BROWS = 8
BCOLS = 32
ALL_TILES = 65536


def clipped_normal(source, salt_value):
    drawn = jax.random.normal(jax.random.fold_in(source, salt_value), (SLIDES, ROWS, COLS, CH), dtype=jnp.float32)
    return jnp.clip(drawn, -5.5, 5.5)


def draw_queries(key, part):
    drawn = clipped_normal(key, 11)
    return drawn.astype(jnp.bfloat16)


def draw_keys(key, part):
    drawn = clipped_normal(key, 12)
    return drawn.astype(jnp.bfloat16)


def draw_occupancy(key, part):
    shape_all = (SLIDES, BROWS, BCOLS)
    filled = jax.random.randint(jax.random.fold_in(key, 21), shape_all, 1, SIDE * SIDE + 1)
    full_pick = jax.random.randint(jax.random.fold_in(key, 22), shape_all, 0, 3) == 0
    slope = (jnp.arange(BCOLS, dtype=jnp.int32) * 4 // BCOLS)[None, None, :]
    empty_pick = jax.random.randint(jax.random.fold_in(key, 23), shape_all, 0, 4) < slope
    counts = jnp.where(full_pick, SIDE * SIDE, filled)
    counts = jnp.where(empty_pick, 0, counts)
    counts = counts.at[:, 0, 0].set(SIDE * SIDE)
    counts = counts.at[:, BROWS - 1, BCOLS - 1].set(0)
    return counts.astype(jnp.int32)


def strengthened(result, stream_key, source, target, blocks, factor):
    def block_of(position):
        return (jnp.arange(result.shape[position]) // (result.shape[position] // blocks)).reshape((-1,) + (1,) * (result.ndim - 1 - position))

    first = jax.random.permutation(stream_key, blocks)[block_of(target)]
    far = (block_of(target) + blocks // 2) % blocks
    return jnp.where((block_of(source) == first) | (block_of(source) == far), factor * result, result)


def level_of(key, shape, split, smallest, largest):
    def one(position, shards_of):
        heights = jax.random.uniform(jax.random.fold_in(jax.random.fold_in(key, 6), position), (shards_of,), jnp.float32, smallest / len(split), largest / len(split))
        return jnp.repeat(jnp.exp(heights), shape[position] // shards_of).reshape((-1,) + (1,) * (len(shape) - position - 1))

    level = one(*split[0])
    for cut in split[1:]:
        level = level * one(*cut)
    return level


def normal_values(stream_key, shape, width, bound, pieces=(), held_as=jnp.bfloat16):
    result = width * jax.random.normal(stream_key, shape, jnp.float32)
    if pieces:
        result = result * level_of(stream_key, shape, pieces, -0.22, 0.18)
    return jnp.clip(result, -bound, bound).astype(held_as)


def heavy_noise(stream_key, extent, scale, bound, shards, heavy, kind=jnp.bfloat16):
    result = scale * jax.random.normal(stream_key, extent, jnp.float32)
    if shards:
        result = result * level_of(stream_key, extent, shards, -0.22, 0.18)
    return jnp.clip(strengthened(result, jax.random.fold_in(stream_key, 3), *heavy), -bound, bound).astype(kind)


def setup_inputs(seed: int = 0) -> dict:
    streams_of = jax.random.split(jax.random.key(seed), 7)
    return {
        "queries": draw_queries(jax.random.fold_in(streams_of[6], 71), 0),
        "keys": draw_keys(jax.random.fold_in(streams_of[6], 71), 0),
        "values": normal_values(streams_of[2], (SLIDES, ROWS, COLS, CH), 1.0, 6.0, ((0, 4), (1, 8), (2, 16))),
        "occupancy": draw_occupancy(jax.random.fold_in(streams_of[6], 71), 0),
        "out_weight": normal_values(streams_of[4], (CH, OUT), CH ** -0.5, 0.21875, ((0, 4),)),
        "grad_out": heavy_noise(streams_of[5], (SLIDES, ROWS, COLS, OUT), 1.0, 6.0, ((0, 4), (1, 8), (2, 16)), (2, 3, 16, 2.0)),
    }


NEG = -1e30


def product(form, left, right):
    return jnp.einsum(form, left.astype(jnp.float32), right.astype(jnp.float32), precision=lax.Precision.HIGHEST)


def near_table(block_side, radius):
    window = block_side + 2 * radius
    queries_at = jnp.arange(block_side * block_side)
    keys_at = jnp.arange(window * window)
    row_gap = keys_at[None, :] // window - queries_at[:, None] // block_side - radius
    col_gap = keys_at[None, :] % window - queries_at[:, None] % block_side - radius
    return (jnp.abs(row_gap) <= radius) & (jnp.abs(col_gap) <= radius)


def tile_valid(counts, block_side):
    inside = jnp.arange(block_side * block_side, dtype=jnp.int32).reshape(block_side, block_side)
    flags = inside[None, :, None, :] < counts[:, None, :, None]
    return flags.reshape(counts.shape[0] * block_side, counts.shape[1] * block_side).astype(jnp.float32)


def blockify(source, block_side):
    height, breadth = source.shape[0], source.shape[1]
    others = source.shape[2:]
    shaped = source.reshape((height // block_side, block_side, breadth // block_side, block_side) + others)
    shaped = jnp.swapaxes(shaped, 1, 2)
    return shaped.reshape((height // block_side, breadth // block_side, block_side * block_side) + others)


def unblock(source, block_side):
    block_rows, block_cols = source.shape[0], source.shape[1]
    others = source.shape[3:]
    shaped = source.reshape((block_rows, block_cols, block_side, block_side) + others)
    shaped = jnp.swapaxes(shaped, 1, 2)
    return shaped.reshape((block_rows * block_side, block_cols * block_side) + others)


def cut_axis(source, dimension, block_side, radius, number):
    padding = [(0, 0)] * source.ndim
    padding[dimension] = (0, block_side - 2 * radius)
    shaped = jnp.pad(source, padding)
    shaped = shaped.reshape(source.shape[:dimension] + (number + 1, block_side) + source.shape[dimension + 1:])
    leading = lax.slice_in_dim(shaped, 0, number, axis=dimension)
    trailing = lax.slice_in_dim(lax.slice_in_dim(shaped, 1, number + 1, axis=dimension), 0, 2 * radius, axis=dimension + 1)
    return jnp.concatenate([leading, trailing], axis=dimension + 1)


def windows(source, block_side, radius, block_rows, block_cols):
    window = block_side + 2 * radius
    shaped = cut_axis(source, 0, block_side, radius, block_rows)
    shaped = cut_axis(shaped, 2, block_side, radius, block_cols)
    shaped = jnp.swapaxes(shaped, 1, 2)
    return shaped.reshape((block_rows * block_cols, window * window) + source.shape[2:])


def merge_axis(source, dimension, block_side, radius, number):
    leading = lax.slice_in_dim(source, 0, block_side, axis=dimension + 1)
    trailing = lax.slice_in_dim(source, block_side, block_side + 2 * radius, axis=dimension + 1)
    lead_pad = [(0, 0)] * source.ndim
    lead_pad[dimension] = (0, 1)
    trail_pad = [(0, 0)] * source.ndim
    trail_pad[dimension] = (1, 0)
    trail_pad[dimension + 1] = (0, block_side - 2 * radius)
    summed = jnp.pad(leading, lead_pad) + jnp.pad(trailing, trail_pad)
    summed = summed.reshape(source.shape[:dimension] + ((number + 1) * block_side,) + source.shape[dimension + 2:])
    return lax.slice_in_dim(summed, 0, number * block_side + 2 * radius, axis=dimension)


def attend(query_blocks, key_win, value_win, key_flag, query_flag, nearby, scaling):
    scores = product("nqhd,nkhd->nhqk", query_blocks, key_win) * scaling
    allowed = nearby[None, None] & (key_flag[:, None, None, :] > 0)
    masked = jnp.where(allowed, scores, NEG)
    highest = jnp.max(masked, axis=-1, keepdims=True)
    raised = jnp.exp(masked - highest)
    inverse = 1.0 / jnp.sum(raised, axis=-1, keepdims=True)
    weights = raised * inverse
    rounded = weights.astype(jnp.bfloat16)
    mixed = product("nhqk,nkhd->nqhd", rounded, value_win)
    attended = (mixed * query_flag[:, :, None, None]).astype(jnp.bfloat16)
    return attended, weights, rounded, highest, inverse


def query_side(weights, rounded, grad_blocks, key_win, value_win, scaling):
    prob_grad = product("nqhd,nkhd->nhqk", grad_blocks, value_win)
    correction = jnp.sum(weights * prob_grad, axis=-1, keepdims=True)
    score_grad = (weights * (prob_grad - correction) * scaling).astype(jnp.bfloat16)
    query_grad = product("nhqk,nkhd->nqhd", score_grad, key_win)
    return query_grad, score_grad, correction


def reference(queries, keys, values, occupancy, out_weight, grad_out):
    nearby = near_table(SIDE, REACH)
    scaling = HEAD_DIM ** -0.5
    window = SIDE + 2 * REACH
    window_area = window * window
    block_area = SIDE * SIDE
    padding = ((REACH, REACH), (REACH, REACH), (0, 0))

    def col_fold(source):
        shaped = source.reshape(1, BCOLS, window, window, CH)
        shaped = jnp.swapaxes(shaped, 1, 2)
        return merge_axis(shaped, 2, SIDE, REACH, BCOLS)[0]

    def one_slide(inputs):
        query_tiles, key_tiles, value_tiles, counts, grad_tiles = inputs
        occupied = tile_valid(counts, SIDE)
        key_ext = jnp.pad(key_tiles, padding)
        value_ext = jnp.pad(value_tiles, padding)
        flag_ext = jnp.pad(occupied.astype(jnp.bfloat16), padding[:2])
        out_back = jnp.dot(grad_tiles.reshape(ROWS * COLS, OUT), out_weight.T, preferred_element_type=jnp.float32)
        gated_grad = out_back.astype(jnp.bfloat16).reshape(ROWS, COLS, CH) * occupied[:, :, None].astype(jnp.bfloat16)
        query_blocks = blockify(query_tiles, SIDE).reshape(BROWS, BCOLS, block_area, HEADS, HEAD_DIM)
        grad_blocks = blockify(gated_grad, SIDE).reshape(BROWS, BCOLS, block_area, HEADS, HEAD_DIM)
        flag_blocks = blockify(occupied, SIDE)
        out_blocks = blockify(grad_tiles, SIDE)

        def one_row(row_index):
            first_row = row_index * SIDE
            key_win = windows(lax.dynamic_slice_in_dim(key_ext, first_row, window, 0), SIDE, REACH, 1, BCOLS)
            key_win = key_win.reshape(BCOLS, window_area, HEADS, HEAD_DIM)
            value_win = windows(lax.dynamic_slice_in_dim(value_ext, first_row, window, 0), SIDE, REACH, 1, BCOLS)
            value_win = value_win.reshape(BCOLS, window_area, HEADS, HEAD_DIM)
            flag_win = windows(lax.dynamic_slice_in_dim(flag_ext, first_row, window, 0), SIDE, REACH, 1, BCOLS)
            row_queries = query_blocks[row_index]
            row_grads = grad_blocks[row_index]
            row_flags = flag_blocks[row_index]
            row_out = out_blocks[row_index]
            attended, weights, rounded, highest, inverse = attend(row_queries, key_win, value_win, flag_win, row_flags, nearby, scaling)
            query_grad, score_grad, correction = query_side(weights, rounded, row_grads, key_win, value_win, scaling)
            key_part = product("nhqk,nqhd->nkhd", score_grad, row_queries)
            value_part = product("nhqk,nqhd->nkhd", rounded, row_grads)
            weight_term = jnp.dot(attended.reshape(BCOLS * block_area, CH).T, row_out.reshape(BCOLS * block_area, OUT), preferred_element_type=jnp.float32)
            return query_grad.reshape(BCOLS, block_area, CH), col_fold(key_part), col_fold(value_part), weight_term

        query_rows, key_rows, value_rows, weight_terms = lax.map(one_row, jnp.arange(BROWS, dtype=jnp.int32))
        grad_query = unblock(query_rows, SIDE)
        key_full = merge_axis(key_rows, 0, SIDE, REACH, BROWS)
        value_full = merge_axis(value_rows, 0, SIDE, REACH, BROWS)
        grad_key = key_full[REACH:REACH + ROWS, REACH:REACH + COLS]
        grad_value = value_full[REACH:REACH + ROWS, REACH:REACH + COLS]
        return (grad_query.astype(jnp.bfloat16), grad_key.astype(jnp.bfloat16), grad_value.astype(jnp.bfloat16), jnp.sum(weight_terms, axis=0))

    grad_queries, grad_keys, grad_values, slide_terms = lax.map(one_slide, (queries, keys, values, occupancy, grad_out))
    grad_weight = jnp.sum(slide_terms, axis=0) * (ALL_TILES ** -0.5)
    return (grad_queries, grad_keys, grad_values, grad_weight)
```

```python
import functools

import jax
import jax.numpy as jnp
import numpy as np
from jax import lax
from jax.experimental import pallas as pl
from jax.experimental.pallas import tpu as pltpu
from jax.sharding import PartitionSpec as P

MESH = pl.DeviceIdType.MESH
CH = 768
SIDE = 8
REACH = 3
HIGH = 8
WIDE = 16
TILES = HIGH * WIDE
PAIR = 128
PAIRS = CH // PAIR
HEAD_SCALE = 64 ** (-0.5)
NEG = -1e30
UP, DOWN, SIDES, KEYS = 128, 176, 224, 320
BF = jnp.bfloat16
F32 = jnp.float32


def key_places():
    places = [(i // WIDE, i % WIDE) for i in range(TILES)]
    places += [(i // WIDE - REACH, i % WIDE) for i in range(48)]
    places += [(i // WIDE + HIGH, i % WIDE) for i in range(48)]
    for first in (-REACH, WIDE):
        places += [(j // 3 - REACH, first + j % 3) if j < 42 else None for j in range(48)]
    return places


@functools.lru_cache(None)
def tables():
    places = key_places()
    limit = np.full((KEYS, TILES), 1000.0, np.float32)
    block = np.zeros((KEYS, 96), np.float32)
    for u, place in enumerate(places):
        if place is None:
            continue
        row, column = place
        block[u, 8 * (4 * (row // SIDE + 1) + column // SIDE + 1)] = 1
        for t in range(TILES):
            if abs(t // WIDE - row) <= REACH and abs(t % WIDE - column) <= REACH:
                limit[u, t] = (row % SIDE) * SIDE + column % SIDE
    pack = np.zeros((96, 2 * TILES), np.float32)
    for kind in range(2):
        for side in range(2):
            for r in range(HIGH):
                for c in range(3):
                    pack[48 * side + 24 * kind + 3 * r + c, TILES * kind + WIDE * r + 13 * side + c] = 1

    def strip(side, kind, r, c):
        return 48 * side + 24 * kind + 3 * r + c

    def corner(kind, side, r, c):
        return 18 * kind + 9 * side + 3 * r + c

    corners = np.zeros((96, 96), np.float32)
    sides = np.zeros((192, 192), np.float32)
    back_corners = np.zeros((96, 192), np.float32)
    back_strips = np.zeros((96, 288), np.float32)
    for kind in range(2):
        for side in range(2):
            for c in range(3):
                for r in range(3):
                    at = corner(kind, side, r, c)
                    corners[at, strip(side, kind, r, c)] = 1
                    corners[48 + at, strip(side, kind, r + 5, c)] = 1
                    sides[96 * kind + 48 * side + 3 * r + c, 96 + at] = 1
                    sides[96 * kind + 48 * side + 3 * (r + 11) + c, 144 + at] = 1
                    back_corners[at, 96 * kind + 48 * side + 3 * r + c] = 1
                    back_corners[48 + at, 96 * kind + 48 * side + 3 * (r + 11) + c] = 1
                    back_strips[strip(side, kind, r, c), 192 + at] = 1
                    back_strips[strip(side, kind, r + 5, c), 192 + 48 + at] = 1
                for r in range(HIGH):
                    sides[96 * kind + 48 * side + 3 * (r + 3) + c, strip(side, kind, r, c)] = 1
                    back_strips[strip(side, kind, r, c), 96 * kind + 48 * side + 3 * (r + 3) + c] = 1
    unpack = np.concatenate([pack[:, :TILES].T, pack[:, TILES:].T], axis=0)
    return tuple(
        np.asarray(t, dtype=BF)
        for t in (limit, block, pack, corners, sides, back_corners, back_strips, unpack)
    )


def dot(a, b, dims=((1,), (0,))):
    return lax.dot_general(a, b, (dims, ((), ())), preferred_element_type=F32)


def body(
    sizes,
    q_ref, k_ref, v_ref, go_ref, w_ref, occ_ref,
    limit_ref, block_ref, pack_ref, corners_ref, sides_ref, bcorn_ref, bstrip_ref, unpack_ref,
    dq_ref, dk_ref, dv_ref, gw_ref,
    kall, vall, strips, held, corn, cnt, wfull, bias, prob, attn_t, gated,
    dk_own, dv_own, row_out, row_in, dcol, bcorn, bcorn_in, bstrip, bstrip_in,
    gw_own, core_out, core_in, y_sum, y_out, y_in, x_sum, x_out, x_in, z_out, z_in, h_all, g_all,
    ssem, rsem,
):
    DP, ROWS, COLS, X = sizes
    Y, ZH = ROWS // 2, COLS // X
    Z = DP * ZH
    part = CH // DP
    half = part // 2
    dp, row, col = lax.axis_index("dp"), lax.axis_index("row"), lax.axis_index("col")
    core, y = row % 2, row // 2
    x, zh = col % X, col // X
    z = zh * DP + dp
    has_up, has_down = row > 0, row < ROWS - 1
    has_left, has_right = col > 0, col < COLS - 1
    up, down = (dp, row - 1, col), (dp, row + 1, col)
    left, right = (dp, row, col - 1), (dp, row, col + 1)
    partner = (dp, row + 1 - 2 * core, col)

    def along_z(step):
        there = (z + step + Z) % Z
        return (there % DP, row, (there // DP) * X + x)

    def along_y(step):
        return (dp, ((y + step) % Y) * 2 + core, col)

    def along_x(step):
        return (dp, row, zh * X + (x + step) % X)

    def along_lo(step):
        return ((dp + step) % DP, row, col)

    def along_hi(step):
        return (dp, row, ((zh + step) % ZH) * X + x)

    if DP == 4:
        plan = [(1, 0, half), (-1, 0, half), (2, 0, half // 2), (-2, half // 2, half // 2)]
    else:
        plan = [(1, 0, half // 2), (-1, half // 2, half // 2)]

    kall[pl.ds(UP, 96), :] = jnp.zeros((96, CH), BF)
    vall[pl.ds(UP, 96), :] = jnp.zeros((96, CH), BF)
    held[...] = jnp.zeros(held.shape, BF)
    row_in[...] = jnp.zeros(row_in.shape, BF)
    bcorn_in[...] = jnp.zeros(bcorn_in.shape, BF)
    bstrip_in[...] = jnp.zeros(bstrip_in.shape, BF)
    cnt[...] = jnp.zeros(cnt.shape, F32)

    barrier = pltpu.get_barrier_semaphore()

    def greet(device):
        pl.semaphore_signal(barrier, inc=1, device_id=device, device_id_type=MESH)

    for there, device in ((has_up, up), (has_down, down), (has_left, left), (has_right, right)):
        pl.when(there)(functools.partial(greet, device))
    fixed = [partner] + [along_z(step) for step, _, _ in plan]
    fixed += [along_y(s) for s in range(1, Y)] + [along_x(s) for s in range(1, X)]
    fixed += [along_lo(s) for s in range(1, DP)] + [along_hi(s) for s in range(1, ZH)]
    for device in fixed:
        greet(device)

    count0, count1 = occ_ref[0, 0].astype(F32), occ_ref[0, 1].astype(F32)
    cnt[1, 1] = jnp.full((8, 128), count0, F32)
    cnt[1, 2] = jnp.full((8, 128), count1, F32)
    packed = dot(pack_ref[:, :TILES], k_ref[...]) + dot(pack_ref[:, TILES:], v_ref[...])
    strips[...] = packed.astype(BF)

    around = sum(t.astype(jnp.int32) for t in (has_up, has_down, has_left, has_right))
    pl.semaphore_wait(barrier, around + len(fixed))

    used = [0]

    class Copy:
        def __init__(self, src, dst, device, sends=None, gets=None):
            index = used[0]
            used[0] += 1
            self.sends, self.gets = sends, gets
            self.copy = pltpu.make_async_remote_copy(
                src_ref=src, dst_ref=dst, send_sem=ssem.at[index], recv_sem=rsem.at[index],
                device_id=device, device_id_type=MESH,
            )

        def start(self):
            if self.sends is None:
                self.copy.start()
            else:
                pl.when(self.sends)(lambda: self.copy.start())
            return self

        def arrived(self):
            if self.gets is None:
                self.copy.wait_recv()
            else:
                pl.when(self.gets)(lambda: self.copy.wait_recv())

        def sent(self):
            if self.sends is None:
                self.copy.wait_send()
            else:
                pl.when(self.sends)(lambda: self.copy.wait_send())

    started = []

    def send(*args, **kwargs):
        made = Copy(*args, **kwargs).start()
        started.append(made)
        return made

    to_left = dict(sends=has_left, gets=has_right)
    to_right = dict(sends=has_right, gets=has_left)
    to_up = dict(sends=has_up, gets=has_down)
    to_down = dict(sends=has_down, gets=has_up)
    first = [
        send(cnt.at[1, 1], cnt.at[1, 3], left, **to_left),
        send(cnt.at[1, 2], cnt.at[1, 0], right, **to_right),
        send(strips.at[pl.ds(0, 48)], held.at[pl.ds(48, 48)], left, **to_left),
        send(strips.at[pl.ds(48, 48)], held.at[pl.ds(0, 48)], right, **to_right),
    ]
    rows = [
        send(k_ref.at[pl.ds(0, 48)], kall.at[pl.ds(DOWN, 48)], up, **to_up),
        send(k_ref.at[pl.ds(80, 48)], kall.at[pl.ds(UP, 48)], down, **to_down),
        send(v_ref.at[pl.ds(0, 48)], vall.at[pl.ds(DOWN, 48)], up, **to_up),
        send(v_ref.at[pl.ds(80, 48)], vall.at[pl.ds(UP, 48)], down, **to_down),
    ]
    kall[pl.ds(0, TILES), :] = k_ref[...]
    vall[pl.ds(0, TILES), :] = v_ref[...]
    base = pl.multiple_of(dp * part, 16)
    wfull[pl.ds(base, part), :] = w_ref[...]

    for copy in first:
        copy.arrived()
    corn[...] = dot(corners_ref[...], held[pl.ds(0, 96), :]).astype(BF)
    second = [
        send(corn.at[pl.ds(0, 48)], held.at[pl.ds(144, 48)], up, **to_up),
        send(corn.at[pl.ds(48, 48)], held.at[pl.ds(96, 48)], down, **to_down),
        send(cnt.at[1], cnt.at[2], up, **to_up),
        send(cnt.at[1], cnt.at[0], down, **to_down),
    ]

    gathers = []
    for step, offset, size in plan:
        own_at = pl.multiple_of(core * half + offset, 16)
        at = pl.multiple_of(dp * part + core * half + offset, 16)
        gathers.append(
            send(w_ref.at[pl.ds(own_at, size)], wfull.at[pl.ds(at, size)], along_z(step))
        )

    for copy in rows + second:
        copy.arrived()
    side_keys = dot(sides_ref[...], held[...])
    kall[pl.ds(SIDES, 96), :] = side_keys[:96].astype(BF)
    vall[pl.ds(SIDES, 96), :] = side_keys[96:].astype(BF)
    counts = dot(block_ref[...], cnt[...].reshape(96, 128).astype(BF))
    near = jnp.where(limit_ref[...].astype(F32) < counts, 0.0, NEG)
    bias[:, :TILES] = near
    bias[:, TILES:] = near

    lane = lax.broadcasted_iota(jnp.int32, (1, 128), 1)
    low = (lane < 64).astype(F32).astype(BF)
    high = (lane >= 64).astype(F32).astype(BF)

    def occupied(index):
        place = ((index >> 4) * 8 + (index & 7)).astype(F32)
        count = jnp.where(((index >> 3) & 1) == 0, count0, count1)
        return (place < count).astype(F32)

    valid_lane = occupied(lane)
    valid_row = occupied(lax.broadcasted_iota(jnp.int32, (TILES, CH), 0))

    def both(value):
        return jnp.concatenate([value * low, value * high], axis=0)

    def own_heads(value):
        return jnp.concatenate([value[:64, :TILES], value[64:, TILES:]], axis=0)

    def lanes(p):
        return pl.ds(pl.multiple_of(p * PAIR, PAIR), PAIR)

    @pl.loop(0, PAIRS)
    def _(p):
        keys, values = kall[:, lanes(p)], vall[:, lanes(p)]
        scores = dot(keys, both(q_ref[:, lanes(p)]), ((1,), (1,))) * HEAD_SCALE + bias[...]
        raised = jnp.exp(scores - jnp.max(scores, axis=0, keepdims=True))
        weights = raised * (1.0 / jnp.sum(raised, axis=0, keepdims=True))
        prob[p] = weights
        mixed = own_heads(dot(values, weights.astype(BF), ((0,), (0,))))
        attn_t[pl.ds(pl.multiple_of(p * PAIR, PAIR), PAIR), :] = (mixed * valid_lane).astype(BF)

    strip_rows = part // Y
    for d in range(DP):
        for j in range(Y):
            at = d * part + j * strip_rows
            term = dot(attn_t[pl.ds(at, strip_rows), :], go_ref[...])
            for c in range(2):
                piece = term[:, c * 384 : (c + 1) * 384]
                gw_own[c, j, d] = piece
                core_out[c, j, d] = piece.astype(BF)
    core_copy = send(core_out.at[1 - core], core_in, partner)

    passed = []
    for copy, (step, offset, size) in zip(gathers, plan):
        copy.arrived()
        source = (dp - step + DP) % DP
        at = pl.multiple_of(source * part + core * half + offset, 16)
        there = wfull.at[pl.ds(at, size)]
        passed.append(send(there, there, partner))
    for copy in passed:
        copy.arrived()
    back = dot(go_ref[...], wfull[...], ((1,), (1,))).astype(BF)
    gated[...] = back * valid_row.astype(BF)

    def backward(p):
        keys, values = kall[:, lanes(p)], vall[:, lanes(p)]
        queries, grads = both(q_ref[:, lanes(p)]), both(gated[:, lanes(p)])
        weights = prob[p]
        prob_grad = dot(values, grads, ((1,), (1,)))
        correction = jnp.sum(weights * prob_grad, axis=0, keepdims=True)
        score_grad = (weights * (prob_grad - correction) * HEAD_SCALE).astype(BF)
        key_part = dot(score_grad, queries)
        value_part = dot(weights.astype(BF), grads)
        dk_own[:, lanes(p)] = key_part[:TILES]
        dv_own[:, lanes(p)] = value_part[:TILES]
        row_out[0, :, lanes(p)] = key_part[UP:DOWN].astype(BF)
        row_out[1, :, lanes(p)] = value_part[UP:DOWN].astype(BF)
        row_out[2, :, lanes(p)] = key_part[DOWN:SIDES].astype(BF)
        row_out[3, :, lanes(p)] = value_part[DOWN:SIDES].astype(BF)
        dcol[pl.ds(0, 96), lanes(p)] = key_part[SIDES:].astype(BF)
        dcol[pl.ds(96, 96), lanes(p)] = value_part[SIDES:].astype(BF)
        query_part = own_heads(dot(keys, score_grad, ((0,), (0,))))
        dq_ref[:, lanes(p)] = query_part.T.astype(BF)

    pl.loop(0, PAIRS // 2)(backward)

    core_copy.arrived()
    total = gw_own[core] + core_in[...].astype(F32)
    y_sum[...] = total
    y_out[...] = total.astype(BF)
    y_copies = [
        send(y_out.at[(y + s) % Y], y_in.at[s - 1], along_y(s)) for s in range(1, Y)
    ]

    pl.loop(PAIRS // 2, PAIRS)(backward)

    bcorn[...] = dot(bcorn_ref[...], dcol[...]).astype(BF)
    back_corners = [
        send(bcorn.at[pl.ds(0, 48)], bcorn_in.at[pl.ds(48, 48)], up, **to_up),
        send(bcorn.at[pl.ds(48, 48)], bcorn_in.at[pl.ds(0, 48)], down, **to_down),
    ]
    back_rows = [
        send(row_out.at[pl.ds(0, 2)], row_in.at[pl.ds(2, 2)], up, **to_up),
        send(row_out.at[pl.ds(2, 2)], row_in.at[pl.ds(0, 2)], down, **to_down),
    ]

    for copy in back_corners:
        copy.arrived()
    returned = dot(bstrip_ref[:, :192], dcol[...]) + dot(bstrip_ref[:, 192:], bcorn_in[...])
    bstrip[...] = returned.astype(BF)
    back_strips = [
        send(bstrip.at[pl.ds(0, 48)], bstrip_in.at[pl.ds(48, 48)], left, **to_left),
        send(bstrip.at[pl.ds(48, 48)], bstrip_in.at[pl.ds(0, 48)], right, **to_right),
    ]

    for copy in y_copies:
        copy.arrived()
    total = y_sum[y]
    for s in range(1, Y):
        total = total + y_in[s - 1].astype(F32)
    x_sum[...] = total
    x_out[...] = total.astype(BF)
    x_copies = [
        send(x_out.at[(x + s) % X], x_in.at[s - 1], along_x(s)) for s in range(1, X)
    ]
    for copy in x_copies:
        copy.arrived()
    total = x_sum[x]
    for s in range(1, X):
        total = total + x_in[s - 1].astype(F32)
    z_out[...] = total.astype(BF)
    keeper = dp == x
    z_copies = []
    for s in range(1, DP):
        z_copies.append(
            send(z_out, z_in.at[s - 1], ((dp + s) % DP, row, col), sends=(dp + s) % DP == x, gets=keeper)
        )
    for copy in z_copies:
        copy.arrived()

    @pl.when(keeper)
    def _():
        gathered = total
        for s in range(1, DP):
            gathered = gathered + z_in[s - 1].astype(F32)
        h_all[zh] = gathered.astype(BF)

    h_copies = [
        send(h_all.at[zh], h_all.at[zh], along_hi(s), sends=keeper, gets=keeper)
        for s in range(1, ZH)
    ]
    for copy in h_copies:
        copy.arrived()

    @pl.when(keeper)
    def _():
        final = h_all[0].astype(F32)
        for s in range(1, ZH):
            final = final + h_all[s].astype(F32)
        g_all[core, y] = final.astype(BF)

    own_piece = g_all.at[core, y]
    spread = [
        send(own_piece, own_piece, along_x(s), sends=keeper, gets=(x + X - s) % X == dp)
        for s in range(1, X)
    ]
    for copy in spread:
        copy.arrived()
    spread_y = [send(own_piece, own_piece, along_y(s)) for s in range(1, Y)]

    for copy in back_rows + back_strips:
        copy.arrived()
    edge = bstrip_in[...]
    for kind, (own, out) in enumerate(((dk_own, dk_ref), (dv_own, dv_ref))):
        side_term = dot(unpack_ref[pl.ds(TILES * kind, TILES), :], edge)
        whole = own[...] + side_term
        top = whole[:48] + row_in[kind].astype(F32)
        bottom = whole[80:] + row_in[2 + kind].astype(F32)
        out[pl.ds(0, 48), :] = top.astype(BF)
        out[pl.ds(48, 32), :] = whole[48:80].astype(BF)
        out[pl.ds(80, 48), :] = bottom.astype(BF)

    for copy in spread_y:
        copy.arrived()
    core_back = send(g_all.at[core], g_all.at[core], partner)
    core_back.arrived()
    norm = (TILES * DP * ROWS * COLS) ** (-0.5)
    for c in range(2):
        for j in range(Y):
            gw_ref[pl.ds(j * strip_rows, strip_rows), pl.ds(c * 384, 384)] = (
                g_all[c, j].astype(F32) * norm
            )
    for copy in started:
        copy.sent()


COPIES = 64


def on_device(sizes, queries, keys, values, occupancy, out_weight, grad_out):
    DP, ROWS, COLS, X = sizes
    Y, ZH = ROWS // 2, COLS // X
    part = CH // DP
    strip_rows = part // Y
    flat = [a.reshape(TILES, CH) for a in (queries, keys, values, grad_out)]
    vmem = pl.BlockSpec(memory_space=pltpu.VMEM)
    piece = (strip_rows, 384)
    scratch = [
        pltpu.VMEM((KEYS, CH), BF),
        pltpu.VMEM((KEYS, CH), BF),
        pltpu.VMEM((96, CH), BF),
        pltpu.VMEM((192, CH), BF),
        pltpu.VMEM((96, CH), BF),
        pltpu.VMEM((3, 4, 8, 128), F32),
        pltpu.VMEM((CH, CH), BF),
        pltpu.VMEM((KEYS, 2 * TILES), F32),
        pltpu.VMEM((PAIRS, KEYS, 2 * TILES), F32),
        pltpu.VMEM((CH, TILES), BF),
        pltpu.VMEM((TILES, CH), BF),
        pltpu.VMEM((TILES, CH), F32),
        pltpu.VMEM((TILES, CH), F32),
        pltpu.VMEM((4, 48, CH), BF),
        pltpu.VMEM((4, 48, CH), BF),
        pltpu.VMEM((192, CH), BF),
        pltpu.VMEM((96, CH), BF),
        pltpu.VMEM((96, CH), BF),
        pltpu.VMEM((96, CH), BF),
        pltpu.VMEM((96, CH), BF),
        pltpu.VMEM((2, Y, DP) + piece, F32),
        pltpu.VMEM((2, Y, DP) + piece, BF),
        pltpu.VMEM((Y, DP) + piece, BF),
        pltpu.VMEM((Y, DP) + piece, F32),
        pltpu.VMEM((Y, DP) + piece, BF),
        pltpu.VMEM((max(Y - 1, 1), DP) + piece, BF),
        pltpu.VMEM((DP,) + piece, F32),
        pltpu.VMEM((DP,) + piece, BF),
        pltpu.VMEM((X - 1,) + piece, BF),
        pltpu.VMEM(piece, BF),
        pltpu.VMEM((DP - 1,) + piece, BF),
        pltpu.VMEM((ZH,) + piece, BF),
        pltpu.VMEM((2, Y) + piece, BF),
        pltpu.SemaphoreType.DMA((COPIES,)),
        pltpu.SemaphoreType.DMA((COPIES,)),
    ]
    tile_out = jax.ShapeDtypeStruct((TILES, CH), BF)
    grad_q, grad_k, grad_v, grad_w = pl.pallas_call(
        functools.partial(body, sizes),
        out_shape=(tile_out, tile_out, tile_out, jax.ShapeDtypeStruct((part, CH), F32)),
        in_specs=[vmem] * 5 + [pl.BlockSpec(memory_space=pltpu.SMEM)] + [vmem] * 8,
        out_specs=(vmem,) * 4,
        scratch_shapes=scratch,
        compiler_params=pltpu.CompilerParams(
            collective_id=0, has_side_effects=True, vmem_limit_bytes=50 * 2**20
        ),
        name="neighbourhood",
    )(*flat, out_weight, occupancy.reshape(1, 2), *(jnp.asarray(t) for t in tables()))
    shape = (1, HIGH, WIDE, CH)
    return grad_q.reshape(shape), grad_k.reshape(shape), grad_v.reshape(shape), grad_w


def solution(mesh):
    dp = mesh.shape["dp"]
    sizes = (dp, mesh.shape["row"], mesh.shape["col"], dp)
    tiles = P("dp", "row", "col", None)
    return jax.shard_map(
        functools.partial(on_device, sizes),
        mesh=mesh,
        in_specs=(tiles, tiles, tiles, P("dp", "row", "col"), P("dp", None), tiles),
        out_specs=(tiles, tiles, tiles, P("dp", None)),
        check_vma=False,
    )
```

```python
import functools

import jax
import jax.numpy as jnp
import numpy as np
from jax import lax
from jax.experimental import pallas as pl
from jax.experimental.pallas import tpu as pltpu
from jax.sharding import PartitionSpec as P

MESH = pl.DeviceIdType.MESH
CH = 768
SIDE = 8
REACH = 3
HIGH = 8
WIDE = 16
TILES = HIGH * WIDE
PAIR = 128
PAIRS = CH // PAIR
HEAD_SCALE = 64 ** (-0.5)
NEG = -1e30
UP, DOWN, SIDES, KEYS = 128, 176, 224, 320
BF = jnp.bfloat16
F32 = jnp.float32


def key_places():
    places = [(i // WIDE, i % WIDE) for i in range(TILES)]
    places += [(i // WIDE - REACH, i % WIDE) for i in range(48)]
    places += [(i // WIDE + HIGH, i % WIDE) for i in range(48)]
    for first in (-REACH, WIDE):
        places += [(j // 3 - REACH, first + j % 3) if j < 42 else None for j in range(48)]
    return places


@functools.lru_cache(None)
def tables():
    places = key_places()
    limit = np.full((KEYS, TILES), 1000.0, np.float32)
    block = np.zeros((KEYS, 96), np.float32)
    for u, place in enumerate(places):
        if place is None:
            continue
        row, column = place
        block[u, 8 * (4 * (row // SIDE + 1) + column // SIDE + 1)] = 1
        for t in range(TILES):
            if abs(t // WIDE - row) <= REACH and abs(t % WIDE - column) <= REACH:
                limit[u, t] = (row % SIDE) * SIDE + column % SIDE
    pack = np.zeros((96, 2 * TILES), np.float32)
    for kind in range(2):
        for side in range(2):
            for r in range(HIGH):
                for c in range(3):
                    pack[48 * side + 24 * kind + 3 * r + c, TILES * kind + WIDE * r + 13 * side + c] = 1

    def strip(side, kind, r, c):
        return 48 * side + 24 * kind + 3 * r + c

    def corner(kind, side, r, c):
        return 18 * kind + 9 * side + 3 * r + c

    corners = np.zeros((96, 96), np.float32)
    sides = np.zeros((192, 192), np.float32)
    back_corners = np.zeros((96, 192), np.float32)
    back_strips = np.zeros((96, 288), np.float32)
    for kind in range(2):
        for side in range(2):
            for c in range(3):
                for r in range(3):
                    at = corner(kind, side, r, c)
                    corners[at, strip(side, kind, r, c)] = 1
                    corners[48 + at, strip(side, kind, r + 5, c)] = 1
                    sides[96 * kind + 48 * side + 3 * r + c, 96 + at] = 1
                    sides[96 * kind + 48 * side + 3 * (r + 11) + c, 144 + at] = 1
                    back_corners[at, 96 * kind + 48 * side + 3 * r + c] = 1
                    back_corners[48 + at, 96 * kind + 48 * side + 3 * (r + 11) + c] = 1
                    back_strips[strip(side, kind, r, c), 192 + at] = 1
                    back_strips[strip(side, kind, r + 5, c), 192 + 48 + at] = 1
                for r in range(HIGH):
                    sides[96 * kind + 48 * side + 3 * (r + 3) + c, strip(side, kind, r, c)] = 1
                    back_strips[strip(side, kind, r, c), 96 * kind + 48 * side + 3 * (r + 3) + c] = 1
    unpack = np.concatenate([pack[:, :TILES].T, pack[:, TILES:].T], axis=0)
    return tuple(
        np.asarray(t, dtype=BF)
        for t in (limit, block, pack, corners, sides, back_corners, back_strips, unpack)
    )


def dot(a, b, dims=((1,), (0,))):
    return lax.dot_general(a, b, (dims, ((), ())), preferred_element_type=F32)


def body(
    sizes,
    q_in, k_in, v_in, go_in, w_in, occ_in,
    limit_in, block_in, pack_in, corners_in, sides_in, bcorn_in_, bstrip_in_, unpack_in,
    dq_ref, dk_ref, dv_ref, gw_ref,
    q_ref, go_ref, w_ref, occ_ref,
    limit_ref, block_ref, pack_ref, corners_ref, sides_ref, bcorn_ref, bstrip_ref, unpack_ref,
    kall, vall, strips, held, corn, cnt, wfull, bias, prob, attn_t, gated,
    dk_own, dv_own, row_out, row_in, dcol, bcorn, bcorn_in, bstrip, bstrip_in,
    gw_own, core_out, core_in, y_sum, y_out, y_in, x_sum, x_out, x_in, z_out, z_in, h_all, g_all,
    ssem, rsem, lsem, far,
):
    DP, ROWS, COLS, X = sizes
    Y, ZH = ROWS // 2, COLS // X
    Z = DP * ZH
    part = CH // DP
    half = part // 2
    dp, row, col = lax.axis_index("dp"), lax.axis_index("row"), lax.axis_index("col")
    core, y = row % 2, row // 2
    x, zh = col % X, col // X
    z = zh * DP + dp
    has_up, has_down = row > 0, row < ROWS - 1
    has_left, has_right = col > 0, col < COLS - 1
    up, down = (dp, row - 1, col), (dp, row + 1, col)
    left, right = (dp, row, col - 1), (dp, row, col + 1)
    partner = (dp, row + 1 - 2 * core, col)

    def along_z(step):
        there = (z + step + Z) % Z
        return (there % DP, row, (there // DP) * X + x)

    def along_y(step):
        return (dp, ((y + step) % Y) * 2 + core, col)

    def along_x(step):
        return (dp, row, zh * X + (x + step) % X)

    def along_lo(step):
        return ((dp + step) % DP, row, col)

    def along_hi(step):
        return (dp, row, ((zh + step) % ZH) * X + x)

    if DP == 4:
        plan = [(1, 0, half), (-1, 0, half), (2, 0, half // 2), (-2, half // 2, half // 2)]
    else:
        plan = [(1, 0, half // 2), (-1, half // 2, half // 2)]

    own = pl.ds(0, TILES)
    loads = [
        (occ_in, occ_ref), (pack_in, pack_ref), (k_in, kall.at[own]), (v_in, vall.at[own]),
        (corners_in, corners_ref), (w_in, w_ref), (sides_in, sides_ref), (block_in, block_ref),
        (limit_in, limit_ref), (q_in, q_ref), (go_in, go_ref), (bcorn_in_, bcorn_ref),
        (bstrip_in_, bstrip_ref), (unpack_in, unpack_ref),
    ]
    loads = [
        pltpu.make_async_copy(src, dst, lsem.at[i]) for i, (src, dst) in enumerate(loads)
    ]
    for load in loads:
        load.start()

    kall[pl.ds(UP, 96), :] = jnp.zeros((96, CH), BF)
    vall[pl.ds(UP, 96), :] = jnp.zeros((96, CH), BF)
    held[...] = jnp.zeros(held.shape, BF)
    row_in[...] = jnp.zeros(row_in.shape, BF)
    bcorn_in[...] = jnp.zeros(bcorn_in.shape, BF)
    bstrip_in[...] = jnp.zeros(bstrip_in.shape, BF)
    cnt[...] = jnp.zeros(cnt.shape, F32)

    barrier = pltpu.get_barrier_semaphore()

    def greet(device):
        pl.semaphore_signal(barrier, inc=1, device_id=device, device_id_type=MESH)

    for there, device in ((has_up, up), (has_down, down), (has_left, left), (has_right, right)):
        pl.when(there)(functools.partial(greet, device))
    fixed = [partner] + [along_z(step) for step, _, _ in plan]
    fixed += [along_y(s) for s in range(1, Y)] + [along_x(s) for s in range(1, X)]
    for device in fixed:
        greet(device)

    for load in loads[:4]:
        load.wait()
    count0, count1 = occ_ref[0, 0].astype(F32), occ_ref[0, 1].astype(F32)
    cnt[1, 1] = jnp.full((8, 128), count0, F32)
    cnt[1, 2] = jnp.full((8, 128), count1, F32)
    packed = dot(pack_ref[:, :TILES], kall[own, :]) + dot(pack_ref[:, TILES:], vall[own, :])
    strips[...] = packed.astype(BF)

    around = sum(t.astype(jnp.int32) for t in (has_up, has_down, has_left, has_right))
    pl.semaphore_wait(barrier, around + len(fixed))

    used = [0]

    class Copy:
        def __init__(self, src, dst, device, sends=None, gets=None):
            index = used[0]
            used[0] += 1
            self.sends, self.gets = sends, gets
            self.copy = pltpu.make_async_remote_copy(
                src_ref=src, dst_ref=dst, send_sem=ssem.at[index], recv_sem=rsem.at[index],
                device_id=device, device_id_type=MESH,
            )

        def start(self):
            if self.sends is None:
                self.copy.start()
            else:
                pl.when(self.sends)(lambda: self.copy.start())
            return self

        def arrived(self):
            if self.gets is None:
                self.copy.wait_recv()
            else:
                pl.when(self.gets)(lambda: self.copy.wait_recv())

        def sent(self):
            if self.sends is None:
                self.copy.wait_send()
            else:
                pl.when(self.sends)(lambda: self.copy.wait_send())

    started = []

    def send(*args, **kwargs):
        made = Copy(*args, **kwargs).start()
        started.append(made)
        return made

    to_left = dict(sends=has_left, gets=has_right)
    to_right = dict(sends=has_right, gets=has_left)
    to_up = dict(sends=has_up, gets=has_down)
    to_down = dict(sends=has_down, gets=has_up)
    first = [
        send(cnt.at[1, 1], cnt.at[1, 3], left, **to_left),
        send(cnt.at[1, 2], cnt.at[1, 0], right, **to_right),
        send(strips.at[pl.ds(0, 48)], held.at[pl.ds(48, 48)], left, **to_left),
        send(strips.at[pl.ds(48, 48)], held.at[pl.ds(0, 48)], right, **to_right),
    ]
    rows = [
        send(kall.at[pl.ds(0, 48)], kall.at[pl.ds(DOWN, 48)], up, **to_up),
        send(kall.at[pl.ds(80, 48)], kall.at[pl.ds(UP, 48)], down, **to_down),
        send(vall.at[pl.ds(0, 48)], vall.at[pl.ds(DOWN, 48)], up, **to_up),
        send(vall.at[pl.ds(80, 48)], vall.at[pl.ds(UP, 48)], down, **to_down),
    ]
    for load in loads[4:]:
        load.wait()
    base = pl.multiple_of(dp * part, 16)
    wfull[pl.ds(base, part), :] = w_ref[...]

    for copy in first:
        copy.arrived()
    corn[...] = dot(corners_ref[...], held[pl.ds(0, 96), :]).astype(BF)
    second = [
        send(corn.at[pl.ds(0, 48)], held.at[pl.ds(144, 48)], up, **to_up),
        send(corn.at[pl.ds(48, 48)], held.at[pl.ds(96, 48)], down, **to_down),
        send(cnt.at[1], cnt.at[2], up, **to_up),
        send(cnt.at[1], cnt.at[0], down, **to_down),
    ]

    gathers = []
    for step, offset, size in plan:
        own_at = pl.multiple_of(core * half + offset, 16)
        at = pl.multiple_of(dp * part + core * half + offset, 16)
        gathers.append(
            send(w_ref.at[pl.ds(own_at, size)], wfull.at[pl.ds(at, size)], along_z(step))
        )

    for copy in rows + second:
        copy.arrived()
    side_keys = dot(sides_ref[...], held[...])
    kall[pl.ds(SIDES, 96), :] = side_keys[:96].astype(BF)
    vall[pl.ds(SIDES, 96), :] = side_keys[96:].astype(BF)
    counts = dot(block_ref[...], cnt[...].reshape(96, 128).astype(BF))
    near = jnp.where(limit_ref[...].astype(F32) < counts, 0.0, NEG)
    bias[:, :TILES] = near
    bias[:, TILES:] = near

    lane = lax.broadcasted_iota(jnp.int32, (1, 128), 1)
    low = (lane < 64).astype(F32).astype(BF)
    high = (lane >= 64).astype(F32).astype(BF)

    def occupied(index):
        place = ((index >> 4) * 8 + (index & 7)).astype(F32)
        count = jnp.where(((index >> 3) & 1) == 0, count0, count1)
        return (place < count).astype(F32)

    valid_lane = occupied(lane)
    valid_row = occupied(lax.broadcasted_iota(jnp.int32, (TILES, CH), 0))

    def both(value):
        return jnp.concatenate([value * low, value * high], axis=0)

    def own_heads(value):
        return jnp.concatenate([value[:64, :TILES], value[64:, TILES:]], axis=0)

    def lanes(p):
        return pl.ds(pl.multiple_of(p * PAIR, PAIR), PAIR)

    @pl.loop(0, PAIRS)
    def _(p):
        keys, values = kall[:, lanes(p)], vall[:, lanes(p)]
        scores = dot(keys, both(q_ref[:, lanes(p)]), ((1,), (1,))) * HEAD_SCALE + bias[...]
        raised = jnp.exp(scores - jnp.max(scores, axis=0, keepdims=True))
        weights = raised * (1.0 / jnp.sum(raised, axis=0, keepdims=True))
        prob[p] = weights
        mixed = own_heads(dot(values, weights.astype(BF), ((0,), (0,))))
        attn_t[pl.ds(pl.multiple_of(p * PAIR, PAIR), PAIR), :] = (mixed * valid_lane).astype(BF)

    strip_rows = part // Y
    for d in range(DP):
        for j in range(Y):
            at = d * part + j * strip_rows
            term = dot(attn_t[pl.ds(at, strip_rows), :], go_ref[...])
            for c in range(2):
                piece = term[:, c * 384 : (c + 1) * 384]
                gw_own[c, j, d] = piece
                core_out[c, j, d] = piece.astype(BF)
    core_copy = send(core_out.at[1 - core], core_in, partner)

    passed = []
    for copy, (step, offset, size) in zip(gathers, plan):
        copy.arrived()
        source = (dp - step + DP) % DP
        at = pl.multiple_of(source * part + core * half + offset, 16)
        there = wfull.at[pl.ds(at, size)]
        passed.append(send(there, there, partner))
    pl.semaphore_signal(far, inc=1, device_id=along_hi(1), device_id_type=MESH)
    for copy in passed:
        copy.arrived()
    back = dot(go_ref[...], wfull[...], ((1,), (1,))).astype(BF)
    gated[...] = back * valid_row.astype(BF)

    core_copy.arrived()
    total = gw_own[core] + core_in[...].astype(F32)
    y_sum[...] = total
    y_out[...] = total.astype(BF)
    y_copies = [
        send(y_out.at[(y + s) % Y], y_in.at[s - 1], along_y(s)) for s in range(1, Y)
    ]

    def backward(p):
        keys, values = kall[:, lanes(p)], vall[:, lanes(p)]
        queries, grads = both(q_ref[:, lanes(p)]), both(gated[:, lanes(p)])
        weights = prob[p]
        prob_grad = dot(values, grads, ((1,), (1,)))
        correction = jnp.sum(weights * prob_grad, axis=0, keepdims=True)
        score_grad = (weights * (prob_grad - correction) * HEAD_SCALE).astype(BF)
        key_part = dot(score_grad, queries)
        value_part = dot(weights.astype(BF), grads)
        dk_own[:, lanes(p)] = key_part[:TILES]
        dv_own[:, lanes(p)] = value_part[:TILES]
        row_out[0, :, lanes(p)] = key_part[UP:DOWN].astype(BF)
        row_out[1, :, lanes(p)] = value_part[UP:DOWN].astype(BF)
        row_out[2, :, lanes(p)] = key_part[DOWN:SIDES].astype(BF)
        row_out[3, :, lanes(p)] = value_part[DOWN:SIDES].astype(BF)
        dcol[pl.ds(0, 96), lanes(p)] = key_part[SIDES:].astype(BF)
        dcol[pl.ds(96, 96), lanes(p)] = value_part[SIDES:].astype(BF)
        query_part = own_heads(dot(keys, score_grad, ((0,), (0,))))
        dq_ref[:, lanes(p)] = query_part.T.astype(BF)

    pl.loop(0, 4)(backward)

    for copy in y_copies:
        copy.arrived()
    total = y_sum[y]
    for s in range(1, Y):
        total = total + y_in[s - 1].astype(F32)
    x_sum[...] = total
    x_out[...] = total.astype(BF)
    x_copies = [
        send(x_out.at[(x + s) % X], x_in.at[s - 1], along_x(s)) for s in range(1, X)
    ]

    pl.loop(4, PAIRS)(backward)

    bcorn[...] = dot(bcorn_ref[...], dcol[...]).astype(BF)
    back_corners = [
        send(bcorn.at[pl.ds(0, 48)], bcorn_in.at[pl.ds(48, 48)], up, **to_up),
        send(bcorn.at[pl.ds(48, 48)], bcorn_in.at[pl.ds(0, 48)], down, **to_down),
    ]
    back_rows = [
        send(row_out.at[pl.ds(0, 2)], row_in.at[pl.ds(2, 2)], up, **to_up),
        send(row_out.at[pl.ds(2, 2)], row_in.at[pl.ds(0, 2)], down, **to_down),
    ]

    for copy in x_copies:
        copy.arrived()
    total = x_sum[x]
    for s in range(1, X):
        total = total + x_in[s - 1].astype(F32)
    z_out[...] = total.astype(BF)
    keeper = dp == x
    z_copies = []
    for s in range(1, DP):
        z_copies.append(
            send(z_out, z_in.at[s - 1], ((dp + s) % DP, row, col), sends=(dp + s) % DP == x, gets=keeper)
        )

    for copy in back_corners:
        copy.arrived()
    returned = dot(bstrip_ref[:, :192], dcol[...]) + dot(bstrip_ref[:, 192:], bcorn_in[...])
    bstrip[...] = returned.astype(BF)
    back_strips = [
        send(bstrip.at[pl.ds(0, 48)], bstrip_in.at[pl.ds(48, 48)], left, **to_left),
        send(bstrip.at[pl.ds(48, 48)], bstrip_in.at[pl.ds(0, 48)], right, **to_right),
    ]

    for copy in z_copies:
        copy.arrived()

    @pl.when(keeper)
    def _():
        gathered = total
        for s in range(1, DP):
            gathered = gathered + z_in[s - 1].astype(F32)
        h_all[zh] = gathered.astype(BF)

    pl.semaphore_wait(far, 1)
    h_copies = [
        send(h_all.at[zh], h_all.at[zh], along_hi(s), sends=keeper, gets=keeper)
        for s in range(1, ZH)
    ]
    for copy in back_rows + back_strips:
        copy.arrived()
    edge = bstrip_in[...]
    for kind, (own, out) in enumerate(((dk_own, dk_ref), (dv_own, dv_ref))):
        side_term = dot(unpack_ref[pl.ds(TILES * kind, TILES), :], edge)
        whole = own[...] + side_term
        top = whole[:48] + row_in[kind].astype(F32)
        bottom = whole[80:] + row_in[2 + kind].astype(F32)
        out[pl.ds(0, 48), :] = top.astype(BF)
        out[pl.ds(48, 32), :] = whole[48:80].astype(BF)
        out[pl.ds(80, 48), :] = bottom.astype(BF)

    for copy in h_copies:
        copy.arrived()

    @pl.when(keeper)
    def _():
        final = h_all[0].astype(F32)
        for s in range(1, ZH):
            final = final + h_all[s].astype(F32)
        g_all[core, y] = final.astype(BF)

    own_piece = g_all.at[core, y]
    spread = [
        send(own_piece, own_piece, along_x(s), sends=keeper, gets=(x + X - s) % X == dp)
        for s in range(1, X)
    ]
    for copy in spread:
        copy.arrived()
    spread_y = [send(own_piece, own_piece, along_y(s)) for s in range(1, Y)]

    for copy in spread_y:
        copy.arrived()
    core_back = send(g_all.at[core], g_all.at[core], partner)
    core_back.arrived()
    norm = (TILES * DP * ROWS * COLS) ** (-0.5)
    for c in range(2):
        for j in range(Y):
            gw_ref[pl.ds(j * strip_rows, strip_rows), pl.ds(c * 384, 384)] = (
                g_all[c, j].astype(F32) * norm
            )
    for copy in started:
        copy.sent()


COPIES = 64


def on_device(sizes, queries, keys, values, occupancy, out_weight, grad_out):
    DP, ROWS, COLS, X = sizes
    Y, ZH = ROWS // 2, COLS // X
    part = CH // DP
    strip_rows = part // Y
    flat = [a.reshape(TILES, CH) for a in (queries, keys, values, grad_out)]
    vmem = pl.BlockSpec(memory_space=pltpu.VMEM)
    hbm = pl.BlockSpec(memory_space=pltpu.HBM)
    fixed = tables()
    piece = (strip_rows, 384)
    scratch = [
        pltpu.VMEM((TILES, CH), BF),
        pltpu.VMEM((TILES, CH), BF),
        pltpu.VMEM((part, CH), BF),
        pltpu.SMEM((1, 2), jnp.int32),
        *(pltpu.VMEM(t.shape, BF) for t in fixed),
        pltpu.VMEM((KEYS, CH), BF),
        pltpu.VMEM((KEYS, CH), BF),
        pltpu.VMEM((96, CH), BF),
        pltpu.VMEM((192, CH), BF),
        pltpu.VMEM((96, CH), BF),
        pltpu.VMEM((3, 4, 8, 128), F32),
        pltpu.VMEM((CH, CH), BF),
        pltpu.VMEM((KEYS, 2 * TILES), F32),
        pltpu.VMEM((PAIRS, KEYS, 2 * TILES), F32),
        pltpu.VMEM((CH, TILES), BF),
        pltpu.VMEM((TILES, CH), BF),
        pltpu.VMEM((TILES, CH), F32),
        pltpu.VMEM((TILES, CH), F32),
        pltpu.VMEM((4, 48, CH), BF),
        pltpu.VMEM((4, 48, CH), BF),
        pltpu.VMEM((192, CH), BF),
        pltpu.VMEM((96, CH), BF),
        pltpu.VMEM((96, CH), BF),
        pltpu.VMEM((96, CH), BF),
        pltpu.VMEM((96, CH), BF),
        pltpu.VMEM((2, Y, DP) + piece, F32),
        pltpu.VMEM((2, Y, DP) + piece, BF),
        pltpu.VMEM((Y, DP) + piece, BF),
        pltpu.VMEM((Y, DP) + piece, F32),
        pltpu.VMEM((Y, DP) + piece, BF),
        pltpu.VMEM((max(Y - 1, 1), DP) + piece, BF),
        pltpu.VMEM((DP,) + piece, F32),
        pltpu.VMEM((DP,) + piece, BF),
        pltpu.VMEM((X - 1,) + piece, BF),
        pltpu.VMEM(piece, BF),
        pltpu.VMEM((DP - 1,) + piece, BF),
        pltpu.VMEM((ZH,) + piece, BF),
        pltpu.VMEM((2, Y) + piece, BF),
        pltpu.SemaphoreType.DMA((COPIES,)),
        pltpu.SemaphoreType.DMA((COPIES,)),
        pltpu.SemaphoreType.DMA((14,)),
        pltpu.SemaphoreType.REGULAR,
    ]
    tile_out = jax.ShapeDtypeStruct((TILES, CH), BF)
    grad_q, grad_k, grad_v, grad_w = pl.pallas_call(
        functools.partial(body, sizes),
        out_shape=(tile_out, tile_out, tile_out, jax.ShapeDtypeStruct((part, CH), F32)),
        in_specs=[hbm] * 14,
        out_specs=(vmem,) * 4,
        scratch_shapes=scratch,
        compiler_params=pltpu.CompilerParams(
            collective_id=0, has_side_effects=True, vmem_limit_bytes=67043328
        ),
        name="neighbourhood",
    )(*flat, out_weight, occupancy.reshape(1, 2), *(jnp.asarray(t) for t in fixed))
    shape = (1, HIGH, WIDE, CH)
    return grad_q.reshape(shape), grad_k.reshape(shape), grad_v.reshape(shape), grad_w


def solution(mesh):
    dp = mesh.shape["dp"]
    sizes = (dp, mesh.shape["row"], mesh.shape["col"], dp)
    tiles = P("dp", "row", "col", None)
    return jax.shard_map(
        functools.partial(on_device, sizes),
        mesh=mesh,
        in_specs=(tiles, tiles, tiles, P("dp", "row", "col"), P("dp", None), tiles),
        out_specs=(tiles, tiles, tiles, P("dp", None)),
        check_vma=False,
    )
```

```python
import functools

import jax
import jax.numpy as jnp
import numpy as np
from jax import lax
from jax.experimental import pallas as pl
from jax.experimental.pallas import tpu as pltpu
from jax.sharding import PartitionSpec as P

MESH = pl.DeviceIdType.MESH
CH = 768
SIDE = 8
REACH = 3
HIGH = 8
WIDE = 16
TILES = HIGH * WIDE
PAIR = 128
PAIRS = CH // PAIR
HEAD_SCALE = 64 ** (-0.5)
NEG = -1e30
UP, DOWN, SIDES, KEYS = 128, 176, 224, 320
BF = jnp.bfloat16
F32 = jnp.float32


def key_places():
    places = [(i // WIDE, i % WIDE) for i in range(TILES)]
    places += [(i // WIDE - REACH, i % WIDE) for i in range(48)]
    places += [(i // WIDE + HIGH, i % WIDE) for i in range(48)]
    for first in (-REACH, WIDE):
        places += [(j // 3 - REACH, first + j % 3) if j < 42 else None for j in range(48)]
    return places


@functools.lru_cache(None)
def tables():
    places = key_places()
    limit = np.full((KEYS, TILES), 1000.0, np.float32)
    block = np.zeros((KEYS, 96), np.float32)
    for u, place in enumerate(places):
        if place is None:
            continue
        row, column = place
        block[u, 8 * (4 * (row // SIDE + 1) + column // SIDE + 1)] = 1
        for t in range(TILES):
            if abs(t // WIDE - row) <= REACH and abs(t % WIDE - column) <= REACH:
                limit[u, t] = (row % SIDE) * SIDE + column % SIDE
    pack = np.zeros((96, 2 * TILES), np.float32)
    for kind in range(2):
        for side in range(2):
            for r in range(HIGH):
                for c in range(3):
                    pack[48 * side + 24 * kind + 3 * r + c, TILES * kind + WIDE * r + 13 * side + c] = 1

    def strip(side, kind, r, c):
        return 48 * side + 24 * kind + 3 * r + c

    def corner(kind, side, r, c):
        return 18 * kind + 9 * side + 3 * r + c

    corners = np.zeros((96, 96), np.float32)
    sides = np.zeros((192, 192), np.float32)
    back_corners = np.zeros((96, 192), np.float32)
    back_strips = np.zeros((96, 288), np.float32)
    for kind in range(2):
        for side in range(2):
            for c in range(3):
                for r in range(3):
                    at = corner(kind, side, r, c)
                    corners[at, strip(side, kind, r, c)] = 1
                    corners[48 + at, strip(side, kind, r + 5, c)] = 1
                    sides[96 * kind + 48 * side + 3 * r + c, 96 + at] = 1
                    sides[96 * kind + 48 * side + 3 * (r + 11) + c, 144 + at] = 1
                    back_corners[at, 96 * kind + 48 * side + 3 * r + c] = 1
                    back_corners[48 + at, 96 * kind + 48 * side + 3 * (r + 11) + c] = 1
                    back_strips[strip(side, kind, r, c), 192 + at] = 1
                    back_strips[strip(side, kind, r + 5, c), 192 + 48 + at] = 1
                for r in range(HIGH):
                    sides[96 * kind + 48 * side + 3 * (r + 3) + c, strip(side, kind, r, c)] = 1
                    back_strips[strip(side, kind, r, c), 96 * kind + 48 * side + 3 * (r + 3) + c] = 1
    unpack = np.concatenate([pack[:, :TILES].T, pack[:, TILES:].T], axis=0)
    return tuple(
        np.asarray(t, dtype=BF)
        for t in (limit, block, pack, corners, sides, back_corners, back_strips, unpack)
    )


def dot(a, b, dims=((1,), (0,))):
    return lax.dot_general(a, b, (dims, ((), ())), preferred_element_type=F32)


def body(
    sizes,
    q_in, k_in, v_in, go_in, w_in, occ_in,
    limit_in, block_in, pack_in, corners_in, sides_in, bcorn_in_, bstrip_in_, unpack_in,
    dq_ref, dk_ref, dv_ref, gw_ref,
    q_ref, go_ref, w_ref, occ_ref,
    limit_ref, block_ref, pack_ref, corners_ref, sides_ref, bcorn_ref, bstrip_ref, unpack_ref,
    kall, vall, strips, held, corn, cnt, wfull, bias, prob, attn_t, gated,
    dk_own, dv_own, row_out, row_in, dcol, bcorn, bcorn_in, bstrip, bstrip_in,
    gw_own, core_out, core_in, xy_sum, y_out, y_in, x_out, x_in, half_sum, half_out, e_in, z_out, z_in, h_all, g_all,
    ssem, rsem, lsem, far,
):
    DP, ROWS, COLS, X = sizes
    Y, ZH = ROWS // 2, COLS // X
    Z = DP * ZH
    part = CH // DP
    half = part // 2
    dp, row, col = lax.axis_index("dp"), lax.axis_index("row"), lax.axis_index("col")
    core, y = row % 2, row // 2
    x, zh = col % X, col // X
    z = zh * DP + dp
    has_up, has_down = row > 0, row < ROWS - 1
    has_left, has_right = col > 0, col < COLS - 1
    up, down = (dp, row - 1, col), (dp, row + 1, col)
    left, right = (dp, row, col - 1), (dp, row, col + 1)
    partner = (dp, row + 1 - 2 * core, col)

    def along_z(step):
        there = (z + step + Z) % Z
        return (there % DP, row, (there // DP) * X + x)

    def along_y(step):
        return (dp, ((y + step) % Y) * 2 + core, col)

    def along_x(step):
        return (dp, row, zh * X + (x + step) % X)

    def along_lo(step):
        return ((dp + step) % DP, row, col)

    def along_hi(step):
        return (dp, row, ((zh + step) % ZH) * X + x)

    if DP == 4:
        plan = [(1, 0, half), (-1, 0, half), (2, 0, half // 2), (-2, half // 2, half // 2)]
    else:
        plan = [(1, 0, half // 2), (-1, half // 2, half // 2)]

    own = pl.ds(0, TILES)
    loads = [
        (occ_in, occ_ref), (pack_in, pack_ref), (k_in, kall.at[own]), (v_in, vall.at[own]),
        (corners_in, corners_ref), (w_in, w_ref), (sides_in, sides_ref), (block_in, block_ref),
        (limit_in, limit_ref), (q_in, q_ref), (go_in, go_ref), (bcorn_in_, bcorn_ref),
        (bstrip_in_, bstrip_ref), (unpack_in, unpack_ref),
    ]
    loads = [
        pltpu.make_async_copy(src, dst, lsem.at[i]) for i, (src, dst) in enumerate(loads)
    ]
    for load in loads:
        load.start()

    kall[pl.ds(UP, 96), :] = jnp.zeros((96, CH), BF)
    vall[pl.ds(UP, 96), :] = jnp.zeros((96, CH), BF)
    held[...] = jnp.zeros(held.shape, BF)
    row_in[...] = jnp.zeros(row_in.shape, BF)
    bcorn_in[...] = jnp.zeros(bcorn_in.shape, BF)
    bstrip_in[...] = jnp.zeros(bstrip_in.shape, BF)
    cnt[...] = jnp.zeros(cnt.shape, F32)

    barrier = pltpu.get_barrier_semaphore()

    def greet(device):
        pl.semaphore_signal(barrier, inc=1, device_id=device, device_id_type=MESH)

    for there, device in ((has_up, up), (has_down, down), (has_left, left), (has_right, right)):
        pl.when(there)(functools.partial(greet, device))
    fixed = [partner] + [along_z(step) for step, _, _ in plan]
    fixed += [along_y(s) for s in range(1, Y)] + [along_x(s) for s in range(1, X)]
    for device in fixed:
        greet(device)

    for load in loads[:4]:
        load.wait()
    count0, count1 = occ_ref[0, 0].astype(F32), occ_ref[0, 1].astype(F32)
    cnt[1, 1] = jnp.full((8, 128), count0, F32)
    cnt[1, 2] = jnp.full((8, 128), count1, F32)
    packed = dot(pack_ref[:, :TILES], kall[own, :]) + dot(pack_ref[:, TILES:], vall[own, :])
    strips[...] = packed.astype(BF)

    around = sum(t.astype(jnp.int32) for t in (has_up, has_down, has_left, has_right))
    pl.semaphore_wait(barrier, around + len(fixed))

    used = [0]

    class Copy:
        def __init__(self, src, dst, device, sends=None, gets=None):
            index = used[0]
            used[0] += 1
            self.sends, self.gets = sends, gets
            self.copy = pltpu.make_async_remote_copy(
                src_ref=src, dst_ref=dst, send_sem=ssem.at[index], recv_sem=rsem.at[index],
                device_id=device, device_id_type=MESH,
            )

        def start(self):
            if self.sends is None:
                self.copy.start()
            else:
                pl.when(self.sends)(lambda: self.copy.start())
            return self

        def arrived(self):
            if self.gets is None:
                self.copy.wait_recv()
            else:
                pl.when(self.gets)(lambda: self.copy.wait_recv())

        def sent(self):
            if self.sends is None:
                self.copy.wait_send()
            else:
                pl.when(self.sends)(lambda: self.copy.wait_send())

    started = []

    def send(*args, **kwargs):
        made = Copy(*args, **kwargs).start()
        started.append(made)
        return made

    to_left = dict(sends=has_left, gets=has_right)
    to_right = dict(sends=has_right, gets=has_left)
    to_up = dict(sends=has_up, gets=has_down)
    to_down = dict(sends=has_down, gets=has_up)
    first = [
        send(cnt.at[1, 1], cnt.at[1, 3], left, **to_left),
        send(cnt.at[1, 2], cnt.at[1, 0], right, **to_right),
        send(strips.at[pl.ds(0, 48)], held.at[pl.ds(48, 48)], left, **to_left),
        send(strips.at[pl.ds(48, 48)], held.at[pl.ds(0, 48)], right, **to_right),
    ]
    rows = [
        send(kall.at[pl.ds(0, 48)], kall.at[pl.ds(DOWN, 48)], up, **to_up),
        send(kall.at[pl.ds(80, 48)], kall.at[pl.ds(UP, 48)], down, **to_down),
        send(vall.at[pl.ds(0, 48)], vall.at[pl.ds(DOWN, 48)], up, **to_up),
        send(vall.at[pl.ds(80, 48)], vall.at[pl.ds(UP, 48)], down, **to_down),
    ]
    for load in loads[4:]:
        load.wait()
    base = pl.multiple_of(dp * part, 16)
    wfull[pl.ds(base, part), :] = w_ref[...]

    for copy in first:
        copy.arrived()
    corn[...] = dot(corners_ref[...], held[pl.ds(0, 96), :]).astype(BF)
    second = [
        send(corn.at[pl.ds(0, 48)], held.at[pl.ds(144, 48)], up, **to_up),
        send(corn.at[pl.ds(48, 48)], held.at[pl.ds(96, 48)], down, **to_down),
        send(cnt.at[1], cnt.at[2], up, **to_up),
        send(cnt.at[1], cnt.at[0], down, **to_down),
    ]

    gathers = []
    for step, offset, size in plan:
        own_at = pl.multiple_of(core * half + offset, 16)
        at = pl.multiple_of(dp * part + core * half + offset, 16)
        gathers.append(
            send(w_ref.at[pl.ds(own_at, size)], wfull.at[pl.ds(at, size)], along_z(step))
        )

    for copy in rows + second:
        copy.arrived()
    side_keys = dot(sides_ref[...], held[...])
    kall[pl.ds(SIDES, 96), :] = side_keys[:96].astype(BF)
    vall[pl.ds(SIDES, 96), :] = side_keys[96:].astype(BF)
    counts = dot(block_ref[...], cnt[...].reshape(96, 128).astype(BF))
    near = jnp.where(limit_ref[...].astype(F32) < counts, 0.0, NEG)
    bias[:, :TILES] = near
    bias[:, TILES:] = near

    lane = lax.broadcasted_iota(jnp.int32, (1, 128), 1)
    low = (lane < 64).astype(F32).astype(BF)
    high = (lane >= 64).astype(F32).astype(BF)

    def occupied(index):
        place = ((index >> 4) * 8 + (index & 7)).astype(F32)
        count = jnp.where(((index >> 3) & 1) == 0, count0, count1)
        return (place < count).astype(F32)

    valid_lane = occupied(lane)
    valid_row = occupied(lax.broadcasted_iota(jnp.int32, (TILES, CH), 0))

    def both(value):
        return jnp.concatenate([value * low, value * high], axis=0)

    def own_heads(value):
        return jnp.concatenate([value[:64, :TILES], value[64:, TILES:]], axis=0)

    def lanes(p):
        if isinstance(p, int):
            return pl.ds(p * PAIR, PAIR)
        return pl.ds(pl.multiple_of(p * PAIR, PAIR), PAIR)

    def forward(p):
        keys, values = kall[:, lanes(p)], vall[:, lanes(p)]
        scores = dot(keys, both(q_ref[:, lanes(p)]), ((1,), (1,))) * HEAD_SCALE + bias[...]
        raised = jnp.exp(scores - jnp.max(scores, axis=0, keepdims=True))
        weights = raised * (1.0 / jnp.sum(raised, axis=0, keepdims=True))
        prob[p] = weights
        mixed = own_heads(dot(values, weights.astype(BF), ((0,), (0,))))
        attn_t[pl.ds(pl.multiple_of(p * PAIR, PAIR), PAIR), :] = (mixed * valid_lane).astype(BF)

    strip_rows = part // Y

    def term_of(h, which):
        columns = pl.ds(pl.multiple_of(which * 384, 128), 384)
        return dot(attn_t[pl.ds(384 * h, 384), :], go_ref[:, columns])

    def cut(term, i, j):
        return term[i * part + j * strip_rows :][:strip_rows]

    core_copies = []
    for h in range(2):
        pl.loop(3 * h, 3 * h + 3)(forward)
        term = term_of(h, 1 - core)
        for j in range(Y):
            for i in range(2):
                core_out[h, j, i] = cut(term, i, j).astype(BF)
        core_copies.append(send(core_out.at[h], core_in.at[h], partner))
        term = term_of(h, core)
        for j in range(Y):
            for i in range(2):
                gw_own[h, j, i] = cut(term, i, j)

    y_copies, x_copies = [], []
    for h in range(2):
        core_copies[h].arrived()
        for j in range(Y):
            for i in range(2):
                d = 2 * h + i
                total = gw_own[h, j, i] + core_in[h, j, i].astype(F32)
                xy_sum[j, d] = total
                if (d + j) % 2 == 0:
                    y_out[h, j] = total.astype(BF)
                else:
                    x_out[d, j // 2] = total.astype(BF)
        for s in range(1, Y):
            y_copies.append(send(y_out.at[h, (y + s) % Y], y_in.at[s - 1, h], along_y(s)))
        for s in range(1, X):
            there = (x + s) % X
            x_copies.append(
                send(x_out.at[there], x_in.at[s - 1], along_x(s), sends=there // 2 == h, gets=x // 2 == h)
            )

    passed = []
    for copy, (step, offset, size) in zip(gathers, plan):
        copy.arrived()
        source = (dp - step + DP) % DP
        at = pl.multiple_of(source * part + core * half + offset, 16)
        there = wfull.at[pl.ds(at, size)]
        passed.append(send(there, there, partner))
    pl.semaphore_signal(far, inc=1, device_id=along_hi(1), device_id_type=MESH)
    for copy in passed:
        copy.arrived()
    back = dot(go_ref[...], wfull[...], ((1,), (1,))).astype(BF)
    gated[...] = back * valid_row.astype(BF)

    def backward(p):
        keys, values = kall[:, lanes(p)], vall[:, lanes(p)]
        queries, grads = both(q_ref[:, lanes(p)]), both(gated[:, lanes(p)])
        weights = prob[p]
        prob_grad = dot(values, grads, ((1,), (1,)))
        correction = jnp.sum(weights * prob_grad, axis=0, keepdims=True)
        score_grad = (weights * (prob_grad - correction) * HEAD_SCALE).astype(BF)
        key_part = dot(score_grad, queries)
        value_part = dot(weights.astype(BF), grads)
        dk_own[:, lanes(p)] = key_part[:TILES]
        dv_own[:, lanes(p)] = value_part[:TILES]
        row_out[0, :, lanes(p)] = key_part[UP:DOWN].astype(BF)
        row_out[1, :, lanes(p)] = value_part[UP:DOWN].astype(BF)
        row_out[2, :, lanes(p)] = key_part[DOWN:SIDES].astype(BF)
        row_out[3, :, lanes(p)] = value_part[DOWN:SIDES].astype(BF)
        dcol[pl.ds(0, 96), lanes(p)] = key_part[SIDES:].astype(BF)
        dcol[pl.ds(96, 96), lanes(p)] = value_part[SIDES:].astype(BF)
        query_part = own_heads(dot(keys, score_grad, ((0,), (0,))))
        dq_ref[:, lanes(p)] = query_part.T.astype(BF)

    def run(first, last):
        if UNROLLED:
            for p in range(first, last):
                backward(p)
        else:
            pl.loop(first, last)(backward)

    run(0, 2)
    for copy in y_copies + x_copies:
        copy.arrived()
    for i in range(2):
        total = xy_sum[y, 2 * i + y % 2]
        for s in range(1, Y):
            total = total + y_in[s - 1, i].astype(F32)
        half_sum[i] = total
        half_out[i] = total.astype(BF)
        total = xy_sum[2 * i + (x + 1) % 2, x]
        for s in range(1, X):
            total = total + x_in[s - 1, i].astype(F32)
        half_sum[2 + i] = total
        half_out[2 + i] = total.astype(BF)
    odd = (x + y) % 2
    second_copies = []
    for s in range(1, X):
        there = (x + s) % X
        second_copies.append(
            send(half_out.at[there // 2], e_in.at[s - 1], along_x(s), sends=(there + y) % 2 == 0, gets=odd == 0)
        )
    for s in range(1, Y):
        there = (y + s) % Y
        second_copies.append(
            send(half_out.at[2 + there // 2], e_in.at[s - 1], along_y(s), sends=(there + x) % 2 == 1, gets=odd == 1)
        )

    run(2, 5)
    for copy in second_copies:
        copy.arrived()
    total = half_sum[odd * (2 + y // 2) + (1 - odd) * (x // 2)]
    for s in range(1, X):
        total = total + e_in[s - 1].astype(F32)
    z_out[...] = total.astype(BF)
    keeper = dp == x
    z_copies = []
    for s in range(1, DP):
        z_copies.append(
            send(z_out, z_in.at[s - 1], ((dp + s) % DP, row, col), sends=(dp + s) % DP == x, gets=keeper)
        )

    run(5, 6)
    bcorn[...] = dot(bcorn_ref[...], dcol[...]).astype(BF)
    back_corners = [
        send(bcorn.at[pl.ds(0, 48)], bcorn_in.at[pl.ds(48, 48)], up, **to_up),
        send(bcorn.at[pl.ds(48, 48)], bcorn_in.at[pl.ds(0, 48)], down, **to_down),
    ]
    back_rows = [
        send(row_out.at[pl.ds(0, 2)], row_in.at[pl.ds(2, 2)], up, **to_up),
        send(row_out.at[pl.ds(2, 2)], row_in.at[pl.ds(0, 2)], down, **to_down),
    ]

    for copy in z_copies:
        copy.arrived()

    @pl.when(keeper)
    def _():
        gathered = total
        for s in range(1, DP):
            gathered = gathered + z_in[s - 1].astype(F32)
        h_all[zh] = gathered.astype(BF)

    pl.semaphore_wait(far, 1)
    h_copies = [
        send(h_all.at[zh], h_all.at[zh], along_hi(s), sends=keeper, gets=keeper)
        for s in range(1, ZH)
    ]
    for copy in back_corners:
        copy.arrived()
    returned = dot(bstrip_ref[:, :192], dcol[...]) + dot(bstrip_ref[:, 192:], bcorn_in[...])
    bstrip[...] = returned.astype(BF)
    back_strips = [
        send(bstrip.at[pl.ds(0, 48)], bstrip_in.at[pl.ds(48, 48)], left, **to_left),
        send(bstrip.at[pl.ds(48, 48)], bstrip_in.at[pl.ds(0, 48)], right, **to_right),
    ]

    for copy in h_copies:
        copy.arrived()

    @pl.when(keeper)
    def _():
        final = h_all[0].astype(F32)
        for s in range(1, ZH):
            final = final + h_all[s].astype(F32)
        g_all[core, y] = final.astype(BF)

    own_piece = g_all.at[core, y]
    spread = [
        send(own_piece, own_piece, along_x(s), sends=keeper, gets=(x + X - s) % X == dp)
        for s in range(1, X)
    ]
    for copy in back_rows:
        copy.arrived()
    for kind, total in enumerate((dk_own, dv_own)):
        total[pl.ds(0, 48), :] += row_in[kind].astype(F32)
        total[pl.ds(80, 48), :] += row_in[2 + kind].astype(F32)

    for copy in spread:
        copy.arrived()
    spread_y = [send(own_piece, own_piece, along_y(s)) for s in range(1, Y)]

    for copy in back_strips:
        copy.arrived()
    edge = bstrip_in[...]
    for kind, (total, out) in enumerate(((dk_own, dk_ref), (dv_own, dv_ref))):
        side_term = dot(unpack_ref[pl.ds(TILES * kind, TILES), :], edge)
        out[...] = (total[...] + side_term).astype(BF)

    for copy in spread_y:
        copy.arrived()
    core_back = send(g_all.at[core], g_all.at[core], partner)
    core_back.arrived()
    norm = (TILES * DP * ROWS * COLS) ** (-0.5)
    for c in range(2):
        for j in range(Y):
            gw_ref[pl.ds(j * strip_rows, strip_rows), pl.ds(c * 384, 384)] = (
                g_all[c, j].astype(F32) * norm
            )
    for copy in started:
        copy.sent()


COPIES = 64
UNROLLED = False
LIMIT = 67043328


def deliver(*refs):
    sources, targets, held, into, out = refs[:4], refs[4:8], refs[8:12], refs[12], refs[13]
    first = [pltpu.make_async_copy(s, h, into.at[i]) for i, (s, h) in enumerate(zip(sources, held))]
    then = [pltpu.make_async_copy(h, t, out.at[i]) for i, (h, t) in enumerate(zip(held, targets))]
    for copy in first:
        copy.start()
    for copy, following in zip(first, then):
        copy.wait()
        following.start()
    for copy in then:
        copy.wait()


def on_device(sizes, queries, keys, values, occupancy, out_weight, grad_out):
    DP, ROWS, COLS, X = sizes
    Y, ZH = ROWS // 2, COLS // X
    part = CH // DP
    strip_rows = part // Y
    flat = [a.reshape(TILES, CH) for a in (queries, keys, values, grad_out)]
    vmem = pl.BlockSpec(memory_space=pltpu.VMEM)
    hbm = pl.BlockSpec(memory_space=pltpu.HBM)
    fixed = tables()
    piece = (strip_rows, 384)
    scratch = [
        pltpu.VMEM((TILES, CH), BF),
        pltpu.VMEM((TILES, CH), BF),
        pltpu.VMEM((part, CH), BF),
        pltpu.SMEM((1, 2), jnp.int32),
        *(pltpu.VMEM(t.shape, BF) for t in fixed),
        pltpu.VMEM((KEYS, CH), BF),
        pltpu.VMEM((KEYS, CH), BF),
        pltpu.VMEM((96, CH), BF),
        pltpu.VMEM((192, CH), BF),
        pltpu.VMEM((96, CH), BF),
        pltpu.VMEM((3, 4, 8, 128), F32),
        pltpu.VMEM((CH, CH), BF),
        pltpu.VMEM((KEYS, 2 * TILES), F32),
        pltpu.VMEM((PAIRS, KEYS, 2 * TILES), F32),
        pltpu.VMEM((CH, TILES), BF),
        pltpu.VMEM((TILES, CH), BF),
        pltpu.VMEM((TILES, CH), F32),
        pltpu.VMEM((TILES, CH), F32),
        pltpu.VMEM((4, 48, CH), BF),
        pltpu.VMEM((4, 48, CH), BF),
        pltpu.VMEM((192, CH), BF),
        pltpu.VMEM((96, CH), BF),
        pltpu.VMEM((96, CH), BF),
        pltpu.VMEM((96, CH), BF),
        pltpu.VMEM((96, CH), BF),
        pltpu.VMEM((2, Y, 2) + piece, F32),
        pltpu.VMEM((2, Y, 2) + piece, BF),
        pltpu.VMEM((2, Y, 2) + piece, BF),
        pltpu.VMEM((Y, DP) + piece, F32),
        pltpu.VMEM((2, Y) + piece, BF),
        pltpu.VMEM((Y - 1, DP // 2) + piece, BF),
        pltpu.VMEM((DP, Y // 2) + piece, BF),
        pltpu.VMEM((X - 1, Y // 2) + piece, BF),
        pltpu.VMEM((4,) + piece, F32),
        pltpu.VMEM((4,) + piece, BF),
        pltpu.VMEM((3,) + piece, BF),
        pltpu.VMEM(piece, BF),
        pltpu.VMEM((DP - 1,) + piece, BF),
        pltpu.VMEM((ZH,) + piece, BF),
        pltpu.VMEM((2, Y) + piece, BF),
        pltpu.SemaphoreType.DMA((COPIES,)),
        pltpu.SemaphoreType.DMA((COPIES,)),
        pltpu.SemaphoreType.DMA((14,)),
        pltpu.SemaphoreType.REGULAR,
    ]
    tile_out = jax.ShapeDtypeStruct((TILES, CH), BF)
    outs = (tile_out, tile_out, tile_out, jax.ShapeDtypeStruct((part, CH), F32))
    made = pl.pallas_call(
        functools.partial(body, sizes),
        out_shape=outs,
        in_specs=[hbm] * 14,
        out_specs=(vmem,) * 4,
        scratch_shapes=scratch,
        compiler_params=pltpu.CompilerParams(
            collective_id=0, has_side_effects=True, vmem_limit_bytes=LIMIT
        ),
        name="neighbourhood",
    )(*flat, out_weight, occupancy.reshape(1, 2), *(jnp.asarray(t) for t in fixed))
    grad_q, grad_k, grad_v, grad_w = pl.pallas_call(
        deliver,
        out_shape=outs,
        in_specs=[hbm] * 4,
        out_specs=(hbm,) * 4,
        scratch_shapes=[pltpu.VMEM(o.shape, o.dtype) for o in outs]
        + [pltpu.SemaphoreType.DMA((4,)), pltpu.SemaphoreType.DMA((4,))],
        compiler_params=pltpu.CompilerParams(vmem_limit_bytes=LIMIT),
        name="deliver",
    )(*made)
    shape = (1, HIGH, WIDE, CH)
    return grad_q.reshape(shape), grad_k.reshape(shape), grad_v.reshape(shape), grad_w


def solution(mesh):
    dp = mesh.shape["dp"]
    sizes = (dp, mesh.shape["row"], mesh.shape["col"], dp)
    tiles = P("dp", "row", "col", None)
    return jax.shard_map(
        functools.partial(on_device, sizes),
        mesh=mesh,
        in_specs=(tiles, tiles, tiles, P("dp", "row", "col"), P("dp", None), tiles),
        out_specs=(tiles, tiles, tiles, P("dp", None)),
        check_vma=False,
    )
```

```python
import functools

import jax
import jax.numpy as jnp
import numpy as np
from jax import lax
from jax.experimental import pallas as pl
from jax.experimental.pallas import tpu as pltpu
from jax.sharding import PartitionSpec as P

MESH = pl.DeviceIdType.MESH
CH = 768
SIDE = 8
REACH = 3
HIGH = 8
WIDE = 16
TILES = HIGH * WIDE
PAIR = 128
PAIRS = CH // PAIR
HEAD_SCALE = 64 ** (-0.5)
NEG = -1e30
UP, DOWN, SIDES, KEYS = 128, 176, 224, 320
BF = jnp.bfloat16
F32 = jnp.float32


def key_places():
    places = [(i // WIDE, i % WIDE) for i in range(TILES)]
    places += [(i // WIDE - REACH, i % WIDE) for i in range(48)]
    places += [(i // WIDE + HIGH, i % WIDE) for i in range(48)]
    for first in (-REACH, WIDE):
        places += [(j // 3 - REACH, first + j % 3) if j < 42 else None for j in range(48)]
    return places


@functools.lru_cache(None)
def tables():
    places = key_places()
    limit = np.full((KEYS, TILES), 1000.0, np.float32)
    block = np.zeros((KEYS, 48), np.float32)
    for u, place in enumerate(places):
        if place is None:
            continue
        row, column = place
        across = column // SIDE if u < SIDES else int(column > 0)
        block[u, 8 * (2 * (row // SIDE + 1) + across)] = 1
        for t in range(TILES):
            if abs(t // WIDE - row) <= REACH and abs(t % WIDE - column) <= REACH:
                limit[u, t] = (row % SIDE) * SIDE + column % SIDE
    pack = np.zeros((96, 2 * TILES), np.float32)
    for kind in range(2):
        for side in range(2):
            for r in range(HIGH):
                for c in range(3):
                    pack[48 * side + 24 * kind + 3 * r + c, TILES * kind + WIDE * r + 13 * side + c] = 1

    def strip(side, kind, r, c):
        return 48 * side + 24 * kind + 3 * r + c

    def corner(kind, side, r, c):
        return 18 * kind + 9 * side + 3 * r + c

    corners = np.zeros((96, 96), np.float32)
    sides = np.zeros((192, 192), np.float32)
    back_corners = np.zeros((96, 192), np.float32)
    back_strips = np.zeros((96, 288), np.float32)
    for kind in range(2):
        for side in range(2):
            for c in range(3):
                for r in range(3):
                    at = corner(kind, side, r, c)
                    corners[at, strip(side, kind, r, c)] = 1
                    corners[48 + at, strip(side, kind, r + 5, c)] = 1
                    sides[96 * kind + 48 * side + 3 * r + c, 96 + at] = 1
                    sides[96 * kind + 48 * side + 3 * (r + 11) + c, 144 + at] = 1
                    back_corners[at, 96 * kind + 48 * side + 3 * r + c] = 1
                    back_corners[48 + at, 96 * kind + 48 * side + 3 * (r + 11) + c] = 1
                    back_strips[strip(side, kind, r, c), 192 + at] = 1
                    back_strips[strip(side, kind, r + 5, c), 192 + 48 + at] = 1
                for r in range(HIGH):
                    sides[96 * kind + 48 * side + 3 * (r + 3) + c, strip(side, kind, r, c)] = 1
                    back_strips[strip(side, kind, r, c), 96 * kind + 48 * side + 3 * (r + 3) + c] = 1
    unpack = np.concatenate([pack[:, :TILES].T, pack[:, TILES:].T], axis=0)
    return tuple(
        np.asarray(t, dtype=BF)
        for t in (limit, block, pack, corners, sides, back_corners, back_strips, unpack)
    )


def dot(a, b, dims=((1,), (0,))):
    return lax.dot_general(a, b, (dims, ((), ())), preferred_element_type=F32)


def body(
    sizes,
    q_in, k_in, v_in, go_in, w_in, occ_in,
    limit_in, block_in, pack_in, corners_in, sides_in, bcorn_in_, bstrip_in_, unpack_in,
    dq_ref, dk_ref, dv_ref, gw_ref,
    q_ref, go_ref, w_ref, occ_ref,
    limit_ref, block_ref, pack_ref, corners_ref, sides_ref, bcorn_ref, bstrip_ref, unpack_ref,
    kall, vall, strips, held, corn, cnt, beside, wfull, bias, prob, peak, mass, attn_t, gated,
    dk_own, dv_own, row_out, row_in, dcol, bcorn, bcorn_in, bstrip, bstrip_in,
    gw_own, core_out, core_in, xy_sum, y_out, y_in, x_out, x_in, half_sum, half_out, e_in, z_out, z_in, h_all, g_all,
    ssem, rsem, lsem, far,
):
    DP, ROWS, COLS, X = sizes
    Y, ZH = ROWS // 2, COLS // X
    Z = DP * ZH
    part = CH // DP
    half = part // 2
    dp, row, col = lax.axis_index("dp"), lax.axis_index("row"), lax.axis_index("col")
    core, y = row % 2, row // 2
    x, zh = col % X, col // X
    z = zh * DP + dp
    has_up, has_down = row > 0, row < ROWS - 1
    has_left, has_right = col > 0, col < COLS - 1
    up, down = (dp, row - 1, col), (dp, row + 1, col)
    left, right = (dp, row, col - 1), (dp, row, col + 1)
    partner = (dp, row + 1 - 2 * core, col)

    def along_z(step):
        there = (z + step + Z) % Z
        return (there % DP, row, (there // DP) * X + x)

    def along_y(step):
        return (dp, ((y + step) % Y) * 2 + core, col)

    def along_x(step):
        return (dp, row, zh * X + (x + step) % X)

    def along_lo(step):
        return ((dp + step) % DP, row, col)

    def along_hi(step):
        return (dp, row, ((zh + step) % ZH) * X + x)

    if DP == 4:
        plan = [(1, 0, half), (-1, 0, half), (2, 0, half // 2), (-2, half // 2, half // 2)]
    else:
        plan = [(1, 0, half // 2), (-1, half // 2, half // 2)]

    own = pl.ds(0, TILES)
    loads = [
        (occ_in, occ_ref), (pack_in, pack_ref), (k_in, kall.at[own]), (v_in, vall.at[own]),
        (corners_in, corners_ref), (w_in, w_ref), (sides_in, sides_ref), (block_in, block_ref),
        (limit_in, limit_ref), (q_in, q_ref), (go_in, go_ref), (bcorn_in_, bcorn_ref),
        (bstrip_in_, bstrip_ref), (unpack_in, unpack_ref),
    ]
    loads = [
        pltpu.make_async_copy(src, dst, lsem.at[i]) for i, (src, dst) in enumerate(loads)
    ]
    for load in loads:
        load.start()

    kall[pl.ds(UP, 96), :] = jnp.zeros((96, CH), BF)
    vall[pl.ds(UP, 96), :] = jnp.zeros((96, CH), BF)
    held[...] = jnp.zeros(held.shape, BF)
    row_in[...] = jnp.zeros(row_in.shape, BF)
    bcorn_in[...] = jnp.zeros(bcorn_in.shape, BF)
    bstrip_in[...] = jnp.zeros(bstrip_in.shape, BF)
    cnt[...] = jnp.zeros(cnt.shape, F32)
    beside[...] = jnp.zeros(beside.shape, F32)

    barrier = pltpu.get_barrier_semaphore()

    def greet(device):
        pl.semaphore_signal(barrier, inc=1, device_id=device, device_id_type=MESH)

    for there, device in ((has_up, up), (has_down, down), (has_left, left), (has_right, right)):
        pl.when(there)(functools.partial(greet, device))
    fixed = [partner] + [along_z(step) for step, _, _ in plan]
    fixed += [along_y(s) for s in range(1, Y)] + [along_x(s) for s in range(1, X)]
    for device in fixed:
        greet(device)

    for load in loads[:4]:
        load.wait()
    count0, count1 = occ_ref[0, 0].astype(F32), occ_ref[0, 1].astype(F32)
    cnt[1, 0] = jnp.full((8, 128), count0, F32)
    cnt[1, 1] = jnp.full((8, 128), count1, F32)
    packed = dot(pack_ref[:, :TILES], kall[own, :]) + dot(pack_ref[:, TILES:], vall[own, :])
    strips[...] = packed.astype(BF)

    around = sum(t.astype(jnp.int32) for t in (has_up, has_down, has_left, has_right))
    pl.semaphore_wait(barrier, around + len(fixed))

    used = [0]

    class Copy:
        def __init__(self, src, dst, device, sends=None, gets=None):
            index = used[0]
            used[0] += 1
            self.sends, self.gets = sends, gets
            self.copy = pltpu.make_async_remote_copy(
                src_ref=src, dst_ref=dst, send_sem=ssem.at[index], recv_sem=rsem.at[index],
                device_id=device, device_id_type=MESH,
            )

        def start(self):
            if self.sends is None:
                self.copy.start()
            else:
                pl.when(self.sends)(lambda: self.copy.start())
            return self

        def arrived(self):
            if self.gets is None:
                self.copy.wait_recv()
            else:
                pl.when(self.gets)(lambda: self.copy.wait_recv())

        def sent(self):
            if self.sends is None:
                self.copy.wait_send()
            else:
                pl.when(self.sends)(lambda: self.copy.wait_send())

    started = []

    def send(*args, **kwargs):
        made = Copy(*args, **kwargs).start()
        started.append(made)
        return made

    to_left = dict(sends=has_left, gets=has_right)
    to_right = dict(sends=has_right, gets=has_left)
    to_up = dict(sends=has_up, gets=has_down)
    to_down = dict(sends=has_down, gets=has_up)
    first = [
        send(cnt.at[1, 0], beside.at[1, 1], left, **to_left),
        send(cnt.at[1, 1], beside.at[1, 0], right, **to_right),
        send(strips.at[pl.ds(0, 48)], held.at[pl.ds(48, 48)], left, **to_left),
        send(strips.at[pl.ds(48, 48)], held.at[pl.ds(0, 48)], right, **to_right),
    ]
    rows = [
        send(cnt.at[1], cnt.at[2], up, **to_up),
        send(cnt.at[1], cnt.at[0], down, **to_down),
        send(kall.at[pl.ds(0, 48)], kall.at[pl.ds(DOWN, 48)], up, **to_up),
        send(kall.at[pl.ds(80, 48)], kall.at[pl.ds(UP, 48)], down, **to_down),
        send(vall.at[pl.ds(0, 48)], vall.at[pl.ds(DOWN, 48)], up, **to_up),
        send(vall.at[pl.ds(80, 48)], vall.at[pl.ds(UP, 48)], down, **to_down),
    ]
    for load in loads[4:]:
        load.wait()
    base = pl.multiple_of(dp * part, 16)
    wfull[pl.ds(base, part), :] = w_ref[...]

    lane = lax.broadcasted_iota(jnp.int32, (1, 128), 1)
    low = (lane < 64).astype(F32).astype(BF)
    high = (lane >= 64).astype(F32).astype(BF)

    def occupied(index):
        place = ((index >> 4) * 8 + (index & 7)).astype(F32)
        count = jnp.where(((index >> 3) & 1) == 0, count0, count1)
        return (place < count).astype(F32)

    valid_lane = occupied(lane)
    valid_row = occupied(lax.broadcasted_iota(jnp.int32, (TILES, CH), 0))

    def both(value):
        return jnp.concatenate([value * low, value * high], axis=0)

    def own_heads(value):
        return jnp.concatenate([value[:64, :TILES], value[64:, TILES:]], axis=0)

    def lanes(p):
        if isinstance(p, int):
            return pl.ds(p * PAIR, PAIR)
        return pl.ds(pl.multiple_of(p * PAIR, PAIR), PAIR)

    for copy in rows:
        copy.arrived()

    def set_bias(first, count, table):
        counts = dot(block_ref[pl.ds(first, count), :], table[...].reshape(48, 128).astype(BF))
        near = jnp.where(limit_ref[pl.ds(first, count), :].astype(F32) < counts, 0.0, NEG)
        bias[pl.ds(first, count), :TILES] = near
        bias[pl.ds(first, count), TILES:] = near

    set_bias(0, SIDES, cnt)

    @pl.loop(0, PAIRS)
    def _(p):
        queries = both(q_ref[:, lanes(p)])
        scores = dot(kall[pl.ds(0, SIDES), lanes(p)], queries, ((1,), (1,))) * HEAD_SCALE + bias[:SIDES, :]
        highest = jnp.max(scores, axis=0, keepdims=True)
        raised = jnp.exp(scores - highest)
        prob[p, :SIDES, :] = raised
        peak[p] = jnp.broadcast_to(highest, (8, 2 * TILES))
        mass[p] = jnp.broadcast_to(jnp.sum(raised, axis=0, keepdims=True), (8, 2 * TILES))

    for copy in first:
        copy.arrived()
    corn[...] = dot(corners_ref[...], held[pl.ds(0, 96), :]).astype(BF)
    second = [
        send(corn.at[pl.ds(0, 48)], held.at[pl.ds(144, 48)], up, **to_up),
        send(corn.at[pl.ds(48, 48)], held.at[pl.ds(96, 48)], down, **to_down),
        send(beside.at[1], beside.at[2], up, **to_up),
        send(beside.at[1], beside.at[0], down, **to_down),
    ]

    gathers = []
    for step, offset, size in plan:
        own_at = pl.multiple_of(core * half + offset, 16)
        at = pl.multiple_of(dp * part + core * half + offset, 16)
        gathers.append(
            send(w_ref.at[pl.ds(own_at, size)], wfull.at[pl.ds(at, size)], along_z(step))
        )

    for copy in second:
        copy.arrived()
    side_keys = dot(sides_ref[...], held[...])
    kall[pl.ds(SIDES, 96), :] = side_keys[:96].astype(BF)
    vall[pl.ds(SIDES, 96), :] = side_keys[96:].astype(BF)
    set_bias(SIDES, KEYS - SIDES, beside)

    def forward(p):
        keys, values = kall[pl.ds(SIDES, KEYS - SIDES), lanes(p)], vall[:, lanes(p)]
        scores = dot(keys, both(q_ref[:, lanes(p)]), ((1,), (1,))) * HEAD_SCALE + bias[SIDES:, :]
        before = peak[p][:1]
        highest = jnp.maximum(before, jnp.max(scores, axis=0, keepdims=True))
        raised = jnp.exp(scores - highest)
        scale = jnp.exp(before - highest)
        inverse = 1.0 / (scale * mass[p][:1] + jnp.sum(raised, axis=0, keepdims=True))
        weights = jnp.concatenate([prob[p, :SIDES, :] * (scale * inverse), raised * inverse], axis=0)
        prob[p] = weights
        mixed = own_heads(dot(values, weights.astype(BF), ((0,), (0,))))
        attn_t[pl.ds(pl.multiple_of(p * PAIR, PAIR), PAIR), :] = (mixed * valid_lane).astype(BF)

    strip_rows = part // Y

    def term_of(h, which):
        columns = pl.ds(pl.multiple_of(which * 384, 128), 384)
        return dot(attn_t[pl.ds(384 * h, 384), :], go_ref[:, columns])

    def cut(term, i, j):
        return term[i * part + j * strip_rows :][:strip_rows]

    core_copies = []
    for h in range(2):
        pl.loop(3 * h, 3 * h + 3)(forward)
        term = term_of(h, 1 - core)
        for j in range(Y):
            for i in range(2):
                core_out[h, j, i] = cut(term, i, j).astype(BF)
        core_copies.append(send(core_out.at[h], core_in.at[h], partner))
        term = term_of(h, core)
        for j in range(Y):
            for i in range(2):
                gw_own[h, j, i] = cut(term, i, j)

    y_copies, x_copies = [], []
    for h in range(2):
        core_copies[h].arrived()
        for j in range(Y):
            for i in range(2):
                d = 2 * h + i
                total = gw_own[h, j, i] + core_in[h, j, i].astype(F32)
                xy_sum[j, d] = total
                if (d + j) % 2 == 0:
                    y_out[h, j] = total.astype(BF)
                else:
                    x_out[d, j // 2] = total.astype(BF)
        for s in range(1, Y):
            y_copies.append(send(y_out.at[h, (y + s) % Y], y_in.at[s - 1, h], along_y(s)))
        for s in range(1, X):
            there = (x + s) % X
            x_copies.append(
                send(x_out.at[there], x_in.at[s - 1], along_x(s), sends=there // 2 == h, gets=x // 2 == h)
            )

    passed = []
    for copy, (step, offset, size) in zip(gathers, plan):
        copy.arrived()
        source = (dp - step + DP) % DP
        at = pl.multiple_of(source * part + core * half + offset, 16)
        there = wfull.at[pl.ds(at, size)]
        passed.append(send(there, there, partner))
    pl.semaphore_signal(far, inc=1, device_id=along_hi(1), device_id_type=MESH)
    for copy in passed:
        copy.arrived()
    back = dot(go_ref[...], wfull[...], ((1,), (1,))).astype(BF)
    gated[...] = back * valid_row.astype(BF)

    def backward(p):
        keys, values = kall[:, lanes(p)], vall[:, lanes(p)]
        queries, grads = both(q_ref[:, lanes(p)]), both(gated[:, lanes(p)])
        weights = prob[p]
        prob_grad = dot(values, grads, ((1,), (1,)))
        correction = jnp.sum(weights * prob_grad, axis=0, keepdims=True)
        score_grad = (weights * (prob_grad - correction) * HEAD_SCALE).astype(BF)
        key_part = dot(score_grad, queries)
        value_part = dot(weights.astype(BF), grads)
        dk_own[:, lanes(p)] = key_part[:TILES]
        dv_own[:, lanes(p)] = value_part[:TILES]
        row_out[0, :, lanes(p)] = key_part[UP:DOWN].astype(BF)
        row_out[1, :, lanes(p)] = value_part[UP:DOWN].astype(BF)
        row_out[2, :, lanes(p)] = key_part[DOWN:SIDES].astype(BF)
        row_out[3, :, lanes(p)] = value_part[DOWN:SIDES].astype(BF)
        dcol[pl.ds(0, 96), lanes(p)] = key_part[SIDES:].astype(BF)
        dcol[pl.ds(96, 96), lanes(p)] = value_part[SIDES:].astype(BF)
        query_part = own_heads(dot(keys, score_grad, ((0,), (0,))))
        dq_ref[:, lanes(p)] = query_part.T.astype(BF)

    def run(first, last):
        if UNROLLED:
            for p in range(first, last):
                backward(p)
        else:
            pl.loop(first, last)(backward)

    run(0, 2)
    for copy in y_copies + x_copies:
        copy.arrived()
    for i in range(2):
        total = xy_sum[y, 2 * i + y % 2]
        for s in range(1, Y):
            total = total + y_in[s - 1, i].astype(F32)
        half_sum[i] = total
        half_out[i] = total.astype(BF)
        total = xy_sum[2 * i + (x + 1) % 2, x]
        for s in range(1, X):
            total = total + x_in[s - 1, i].astype(F32)
        half_sum[2 + i] = total
        half_out[2 + i] = total.astype(BF)
    odd = (x + y) % 2
    second_copies = []
    for s in range(1, X):
        there = (x + s) % X
        second_copies.append(
            send(half_out.at[there // 2], e_in.at[s - 1], along_x(s), sends=(there + y) % 2 == 0, gets=odd == 0)
        )
    for s in range(1, Y):
        there = (y + s) % Y
        second_copies.append(
            send(half_out.at[2 + there // 2], e_in.at[s - 1], along_y(s), sends=(there + x) % 2 == 1, gets=odd == 1)
        )

    run(2, 5)
    for copy in second_copies:
        copy.arrived()
    total = half_sum[odd * (2 + y // 2) + (1 - odd) * (x // 2)]
    for s in range(1, X):
        total = total + e_in[s - 1].astype(F32)
    z_out[...] = total.astype(BF)
    keeper = dp == x
    behind = (z + Z - x) % DP
    z_copies = [
        send(z_out, z_in.at[i], along_z(step), sends=behind == (DP - step) % DP, gets=keeper)
        for i, step in enumerate((-1, 1, -2))
    ]

    run(5, 6)
    bcorn[...] = dot(bcorn_ref[...], dcol[...]).astype(BF)
    back_corners = [
        send(bcorn.at[pl.ds(0, 48)], bcorn_in.at[pl.ds(48, 48)], up, **to_up),
        send(bcorn.at[pl.ds(48, 48)], bcorn_in.at[pl.ds(0, 48)], down, **to_down),
    ]
    back_rows = [
        send(row_out.at[pl.ds(0, 2)], row_in.at[pl.ds(2, 2)], up, **to_up),
        send(row_out.at[pl.ds(2, 2)], row_in.at[pl.ds(0, 2)], down, **to_down),
    ]

    for copy in z_copies:
        copy.arrived()

    @pl.when(keeper)
    def _():
        gathered = total
        for s in range(1, DP):
            gathered = gathered + z_in[s - 1].astype(F32)
        h_all[zh] = gathered.astype(BF)

    pl.semaphore_wait(far, 1)
    h_copies = [
        send(h_all.at[zh], h_all.at[zh], along_hi(s), sends=keeper, gets=keeper)
        for s in range(1, ZH)
    ]
    for copy in back_corners:
        copy.arrived()
    returned = dot(bstrip_ref[:, :192], dcol[...]) + dot(bstrip_ref[:, 192:], bcorn_in[...])
    bstrip[...] = returned.astype(BF)
    back_strips = [
        send(bstrip.at[pl.ds(0, 48)], bstrip_in.at[pl.ds(48, 48)], left, **to_left),
        send(bstrip.at[pl.ds(48, 48)], bstrip_in.at[pl.ds(0, 48)], right, **to_right),
    ]

    for copy in h_copies:
        copy.arrived()

    @pl.when(keeper)
    def _():
        final = h_all[0].astype(F32)
        for s in range(1, ZH):
            final = final + h_all[s].astype(F32)
        g_all[core, y] = final.astype(BF)

    own_piece = g_all.at[core, y]
    spread = [
        send(own_piece, own_piece, along_x(s), sends=keeper, gets=(x + X - s) % X == dp)
        for s in range(1, X)
    ]
    for copy in back_rows:
        copy.arrived()
    for kind, total in enumerate((dk_own, dv_own)):
        total[pl.ds(0, 48), :] += row_in[kind].astype(F32)
        total[pl.ds(80, 48), :] += row_in[2 + kind].astype(F32)

    for copy in spread:
        copy.arrived()
    spread_y = [send(own_piece, own_piece, along_y(s)) for s in range(1, Y)]

    for copy in back_strips:
        copy.arrived()
    edge = bstrip_in[...]
    for kind, (total, out) in enumerate(((dk_own, dk_ref), (dv_own, dv_ref))):
        side_term = dot(unpack_ref[pl.ds(TILES * kind, TILES), :], edge)
        out[...] = (total[...] + side_term).astype(BF)

    for copy in spread_y:
        copy.arrived()
    core_back = send(g_all.at[core], g_all.at[core], partner)
    core_back.arrived()
    norm = (TILES * DP * ROWS * COLS) ** (-0.5)
    for c in range(2):
        for j in range(Y):
            gw_ref[pl.ds(j * strip_rows, strip_rows), pl.ds(c * 384, 384)] = (
                g_all[c, j].astype(F32) * norm
            )
    for copy in started:
        copy.sent()


COPIES = 64
UNROLLED = False
LIMIT = 67043328


def deliver(*refs):
    sources, targets, held, into, out = refs[:4], refs[4:8], refs[8:12], refs[12], refs[13]
    first = [pltpu.make_async_copy(s, h, into.at[i]) for i, (s, h) in enumerate(zip(sources, held))]
    then = [pltpu.make_async_copy(h, t, out.at[i]) for i, (h, t) in enumerate(zip(held, targets))]
    for copy in first:
        copy.start()
    for copy, following in zip(first, then):
        copy.wait()
        following.start()
    for copy in then:
        copy.wait()


def on_device(sizes, queries, keys, values, occupancy, out_weight, grad_out):
    DP, ROWS, COLS, X = sizes
    Y, ZH = ROWS // 2, COLS // X
    part = CH // DP
    strip_rows = part // Y
    flat = [a.reshape(TILES, CH) for a in (queries, keys, values, grad_out)]
    vmem = pl.BlockSpec(memory_space=pltpu.VMEM)
    hbm = pl.BlockSpec(memory_space=pltpu.HBM)
    fixed = tables()
    piece = (strip_rows, 384)
    scratch = [
        pltpu.VMEM((TILES, CH), BF),
        pltpu.VMEM((TILES, CH), BF),
        pltpu.VMEM((part, CH), BF),
        pltpu.SMEM((1, 2), jnp.int32),
        *(pltpu.VMEM(t.shape, BF) for t in fixed),
        pltpu.VMEM((KEYS, CH), BF),
        pltpu.VMEM((KEYS, CH), BF),
        pltpu.VMEM((96, CH), BF),
        pltpu.VMEM((192, CH), BF),
        pltpu.VMEM((96, CH), BF),
        pltpu.VMEM((3, 2, 8, 128), F32),
        pltpu.VMEM((3, 2, 8, 128), F32),
        pltpu.VMEM((CH, CH), BF),
        pltpu.VMEM((KEYS, 2 * TILES), F32),
        pltpu.VMEM((PAIRS, KEYS, 2 * TILES), F32),
        pltpu.VMEM((PAIRS, 8, 2 * TILES), F32),
        pltpu.VMEM((PAIRS, 8, 2 * TILES), F32),
        pltpu.VMEM((CH, TILES), BF),
        pltpu.VMEM((TILES, CH), BF),
        pltpu.VMEM((TILES, CH), F32),
        pltpu.VMEM((TILES, CH), F32),
        pltpu.VMEM((4, 48, CH), BF),
        pltpu.VMEM((4, 48, CH), BF),
        pltpu.VMEM((192, CH), BF),
        pltpu.VMEM((96, CH), BF),
        pltpu.VMEM((96, CH), BF),
        pltpu.VMEM((96, CH), BF),
        pltpu.VMEM((96, CH), BF),
        pltpu.VMEM((2, Y, 2) + piece, F32),
        pltpu.VMEM((2, Y, 2) + piece, BF),
        pltpu.VMEM((2, Y, 2) + piece, BF),
        pltpu.VMEM((Y, DP) + piece, F32),
        pltpu.VMEM((2, Y) + piece, BF),
        pltpu.VMEM((Y - 1, DP // 2) + piece, BF),
        pltpu.VMEM((DP, Y // 2) + piece, BF),
        pltpu.VMEM((X - 1, Y // 2) + piece, BF),
        pltpu.VMEM((4,) + piece, F32),
        pltpu.VMEM((4,) + piece, BF),
        pltpu.VMEM((3,) + piece, BF),
        pltpu.VMEM(piece, BF),
        pltpu.VMEM((DP - 1,) + piece, BF),
        pltpu.VMEM((ZH,) + piece, BF),
        pltpu.VMEM((2, Y) + piece, BF),
        pltpu.SemaphoreType.DMA((COPIES,)),
        pltpu.SemaphoreType.DMA((COPIES,)),
        pltpu.SemaphoreType.DMA((14,)),
        pltpu.SemaphoreType.REGULAR,
    ]
    tile_out = jax.ShapeDtypeStruct((TILES, CH), BF)
    outs = (tile_out, tile_out, tile_out, jax.ShapeDtypeStruct((part, CH), F32))
    made = pl.pallas_call(
        functools.partial(body, sizes),
        out_shape=outs,
        in_specs=[hbm] * 14,
        out_specs=(vmem,) * 4,
        scratch_shapes=scratch,
        compiler_params=pltpu.CompilerParams(
            collective_id=0, has_side_effects=True, vmem_limit_bytes=LIMIT
        ),
        name="neighbourhood",
    )(*flat, out_weight, occupancy.reshape(1, 2), *(jnp.asarray(t) for t in fixed))
    grad_q, grad_k, grad_v, grad_w = pl.pallas_call(
        deliver,
        out_shape=outs,
        in_specs=[hbm] * 4,
        out_specs=(hbm,) * 4,
        scratch_shapes=[pltpu.VMEM(o.shape, o.dtype) for o in outs]
        + [pltpu.SemaphoreType.DMA((4,)), pltpu.SemaphoreType.DMA((4,))],
        compiler_params=pltpu.CompilerParams(vmem_limit_bytes=LIMIT),
        name="deliver",
    )(*made)
    shape = (1, HIGH, WIDE, CH)
    return grad_q.reshape(shape), grad_k.reshape(shape), grad_v.reshape(shape), grad_w


def solution(mesh):
    dp = mesh.shape["dp"]
    sizes = (dp, mesh.shape["row"], mesh.shape["col"], dp)
    tiles = P("dp", "row", "col", None)
    return jax.shard_map(
        functools.partial(on_device, sizes),
        mesh=mesh,
        in_specs=(tiles, tiles, tiles, P("dp", "row", "col"), P("dp", None), tiles),
        out_specs=(tiles, tiles, tiles, P("dp", None)),
        check_vma=False,
    )
```

```python
import functools

import jax
import jax.numpy as jnp
import numpy as np
from jax import lax
from jax.experimental import pallas as pl
from jax.experimental.pallas import tpu as pltpu
from jax.sharding import PartitionSpec as P

MESH = pl.DeviceIdType.MESH
CH = 768
SIDE = 8
REACH = 3
HIGH = 8
WIDE = 16
TILES = HIGH * WIDE
PAIR = 128
PAIRS = CH // PAIR
HEAD_SCALE = 64 ** (-0.5)
NEG = -1e30
UP, DOWN, SIDES, KEYS = 128, 176, 224, 320
BF = jnp.bfloat16
F32 = jnp.float32


def key_places():
    places = [(i // WIDE, i % WIDE) for i in range(TILES)]
    places += [(i // WIDE - REACH, i % WIDE) for i in range(48)]
    places += [(i // WIDE + HIGH, i % WIDE) for i in range(48)]
    for first in (-REACH, WIDE):
        places += [(j // 3 - REACH, first + j % 3) if j < 42 else None for j in range(48)]
    return places


@functools.lru_cache(None)
def tables():
    places = key_places()
    limit = np.full((KEYS, TILES), 1000.0, np.float32)
    block = np.zeros((KEYS, 48), np.float32)
    for u, place in enumerate(places):
        if place is None:
            continue
        row, column = place
        across = column // SIDE if u < SIDES else int(column > 0)
        block[u, 8 * (2 * (row // SIDE + 1) + across)] = 1
        for t in range(TILES):
            if abs(t // WIDE - row) <= REACH and abs(t % WIDE - column) <= REACH:
                limit[u, t] = (row % SIDE) * SIDE + column % SIDE
    pack = np.zeros((96, 2 * TILES), np.float32)
    for kind in range(2):
        for side in range(2):
            for r in range(HIGH):
                for c in range(3):
                    pack[48 * side + 24 * kind + 3 * r + c, TILES * kind + WIDE * r + 13 * side + c] = 1

    def strip(side, kind, r, c):
        return 48 * side + 24 * kind + 3 * r + c

    def corner(kind, side, r, c):
        return 18 * kind + 9 * side + 3 * r + c

    corners = np.zeros((96, 96), np.float32)
    sides = np.zeros((192, 192), np.float32)
    back_corners = np.zeros((96, 192), np.float32)
    back_strips = np.zeros((96, 288), np.float32)
    for kind in range(2):
        for side in range(2):
            for c in range(3):
                for r in range(3):
                    at = corner(kind, side, r, c)
                    corners[at, strip(side, kind, r, c)] = 1
                    corners[48 + at, strip(side, kind, r + 5, c)] = 1
                    sides[96 * kind + 48 * side + 3 * r + c, 96 + at] = 1
                    sides[96 * kind + 48 * side + 3 * (r + 11) + c, 144 + at] = 1
                    back_corners[at, 96 * kind + 48 * side + 3 * r + c] = 1
                    back_corners[48 + at, 96 * kind + 48 * side + 3 * (r + 11) + c] = 1
                    back_strips[strip(side, kind, r, c), 192 + at] = 1
                    back_strips[strip(side, kind, r + 5, c), 192 + 48 + at] = 1
                for r in range(HIGH):
                    sides[96 * kind + 48 * side + 3 * (r + 3) + c, strip(side, kind, r, c)] = 1
                    back_strips[strip(side, kind, r, c), 96 * kind + 48 * side + 3 * (r + 3) + c] = 1
    unpack = np.concatenate([pack[:, :TILES].T, pack[:, TILES:].T], axis=0)
    return tuple(
        np.asarray(t, dtype=BF)
        for t in (limit, block, pack, corners, sides, back_corners, back_strips, unpack)
    )


def dot(a, b, dims=((1,), (0,))):
    return lax.dot_general(a, b, (dims, ((), ())), preferred_element_type=F32)


def body(
    sizes,
    q_in, k_in, v_in, go_in, w_in, occ_in,
    limit_in, block_in, pack_in, corners_in, sides_in, bcorn_in_, bstrip_in_, unpack_in,
    dq_ref, dk_ref, dv_ref, gw_ref,
    q_ref, go_ref, w_ref, occ_ref,
    limit_ref, block_ref, pack_ref, corners_ref, sides_ref, bcorn_ref, bstrip_ref, unpack_ref,
    kall, vall, strips, held, corn, cnt, beside, wfull, bias, prob, peak, mass, attn_t, gated,
    dk_own, dv_own, row_out, row_in, dcol, bcorn, bcorn_in, bstrip, bstrip_in,
    gw_own, core_out, core_in, xy_sum, y_out, y_in, x_out, x_in, half_sum, half_out, e_in, z_out, z_in, h_all, g_all,
    ssem, rsem, lsem, far,
):
    DP, ROWS, COLS, X = sizes
    Y, ZH = ROWS // 2, COLS // X
    Z = DP * ZH
    part = CH // DP
    half = part // 2
    dp, row, col = lax.axis_index("dp"), lax.axis_index("row"), lax.axis_index("col")
    core, y = row % 2, row // 2
    x, zh = col % X, col // X
    z = zh * DP + dp
    has_up, has_down = row > 0, row < ROWS - 1
    has_left, has_right = col > 0, col < COLS - 1
    up, down = (dp, row - 1, col), (dp, row + 1, col)
    left, right = (dp, row, col - 1), (dp, row, col + 1)
    partner = (dp, row + 1 - 2 * core, col)

    def along_z(step):
        there = (z + step + Z) % Z
        return (there % DP, row, (there // DP) * X + x)

    def along_y(step):
        return (dp, ((y + step) % Y) * 2 + core, col)

    def along_x(step):
        return (dp, row, zh * X + (x + step) % X)

    def along_lo(step):
        return ((dp + step) % DP, row, col)

    def along_hi(step):
        return (dp, row, ((zh + step) % ZH) * X + x)

    if DP == 4:
        plan = [(1, 0, half), (-1, 0, half), (2, 0, half // 2), (-2, half // 2, half // 2)]
    else:
        plan = [(1, 0, half // 2), (-1, half // 2, half // 2)]

    own = pl.ds(0, TILES)
    loads = [
        (occ_in, occ_ref), (pack_in, pack_ref), (k_in, kall.at[own]), (v_in, vall.at[own]),
        (corners_in, corners_ref), (w_in, w_ref), (sides_in, sides_ref), (block_in, block_ref),
        (limit_in, limit_ref), (q_in, q_ref), (go_in, go_ref), (bcorn_in_, bcorn_ref),
        (bstrip_in_, bstrip_ref), (unpack_in, unpack_ref),
    ]
    loads = [
        pltpu.make_async_copy(src, dst, lsem.at[i]) for i, (src, dst) in enumerate(loads)
    ]
    for load in loads:
        load.start()

    kall[pl.ds(UP, 96), :] = jnp.zeros((96, CH), BF)
    vall[pl.ds(UP, 96), :] = jnp.zeros((96, CH), BF)
    held[...] = jnp.zeros(held.shape, BF)
    row_in[...] = jnp.zeros(row_in.shape, BF)
    bcorn_in[...] = jnp.zeros(bcorn_in.shape, BF)
    bstrip_in[...] = jnp.zeros(bstrip_in.shape, BF)
    cnt[...] = jnp.zeros(cnt.shape, F32)
    beside[...] = jnp.zeros(beside.shape, F32)

    barrier = pltpu.get_barrier_semaphore()

    def greet(device):
        pl.semaphore_signal(barrier, inc=1, device_id=device, device_id_type=MESH)

    for there, device in ((has_up, up), (has_down, down), (has_left, left), (has_right, right)):
        pl.when(there)(functools.partial(greet, device))
    fixed = [partner] + [along_z(step) for step, _, _ in plan]
    fixed += [along_y(s) for s in range(1, Y)] + [along_x(s) for s in range(1, X)]
    for device in fixed:
        greet(device)

    for load in loads[:4]:
        load.wait()
    count0, count1 = occ_ref[0, 0].astype(F32), occ_ref[0, 1].astype(F32)
    cnt[1, 0] = jnp.full((8, 128), count0, F32)
    cnt[1, 1] = jnp.full((8, 128), count1, F32)
    packed = dot(pack_ref[:, :TILES], kall[own, :]) + dot(pack_ref[:, TILES:], vall[own, :])
    strips[...] = packed.astype(BF)

    around = sum(t.astype(jnp.int32) for t in (has_up, has_down, has_left, has_right))
    pl.semaphore_wait(barrier, around + len(fixed))

    used = [0]

    class Copy:
        def __init__(self, src, dst, device, sends=None, gets=None):
            index = used[0]
            used[0] += 1
            self.sends, self.gets = sends, gets
            self.copy = pltpu.make_async_remote_copy(
                src_ref=src, dst_ref=dst, send_sem=ssem.at[index], recv_sem=rsem.at[index],
                device_id=device, device_id_type=MESH,
            )

        def start(self):
            if self.sends is None:
                self.copy.start()
            else:
                pl.when(self.sends)(lambda: self.copy.start())
            return self

        def arrived(self):
            if self.gets is None:
                self.copy.wait_recv()
            else:
                pl.when(self.gets)(lambda: self.copy.wait_recv())

        def sent(self):
            if self.sends is None:
                self.copy.wait_send()
            else:
                pl.when(self.sends)(lambda: self.copy.wait_send())

    started = []

    def send(*args, **kwargs):
        made = Copy(*args, **kwargs).start()
        started.append(made)
        return made

    to_left = dict(sends=has_left, gets=has_right)
    to_right = dict(sends=has_right, gets=has_left)
    to_up = dict(sends=has_up, gets=has_down)
    to_down = dict(sends=has_down, gets=has_up)
    first = [
        send(cnt.at[1, 0], beside.at[1, 1], left, **to_left),
        send(cnt.at[1, 1], beside.at[1, 0], right, **to_right),
        send(strips.at[pl.ds(0, 48)], held.at[pl.ds(48, 48)], left, **to_left),
        send(strips.at[pl.ds(48, 48)], held.at[pl.ds(0, 48)], right, **to_right),
    ]
    rows = [
        send(cnt.at[1], cnt.at[2], up, **to_up),
        send(cnt.at[1], cnt.at[0], down, **to_down),
        send(kall.at[pl.ds(0, 48)], kall.at[pl.ds(DOWN, 48)], up, **to_up),
        send(kall.at[pl.ds(80, 48)], kall.at[pl.ds(UP, 48)], down, **to_down),
        send(vall.at[pl.ds(0, 48)], vall.at[pl.ds(DOWN, 48)], up, **to_up),
        send(vall.at[pl.ds(80, 48)], vall.at[pl.ds(UP, 48)], down, **to_down),
    ]
    for load in loads[4:]:
        load.wait()
    base = pl.multiple_of(dp * part, 16)
    wfull[pl.ds(base, part), :] = w_ref[...]

    lane = lax.broadcasted_iota(jnp.int32, (1, 128), 1)
    low = (lane < 64).astype(F32).astype(BF)
    high = (lane >= 64).astype(F32).astype(BF)

    def occupied(index):
        place = ((index >> 4) * 8 + (index & 7)).astype(F32)
        count = jnp.where(((index >> 3) & 1) == 0, count0, count1)
        return (place < count).astype(F32)

    valid_lane = occupied(lane)
    valid_row = occupied(lax.broadcasted_iota(jnp.int32, (TILES, CH), 0))

    def both(value):
        return jnp.concatenate([value * low, value * high], axis=0)

    def own_heads(value):
        return jnp.concatenate([value[:64, :TILES], value[64:, TILES:]], axis=0)

    def lanes(p):
        if isinstance(p, int):
            return pl.ds(p * PAIR, PAIR)
        return pl.ds(pl.multiple_of(p * PAIR, PAIR), PAIR)

    for copy in rows:
        copy.arrived()

    def set_bias(first, count, table):
        counts = dot(block_ref[pl.ds(first, count), :], table[...].reshape(48, 128).astype(BF))
        near = jnp.where(limit_ref[pl.ds(first, count), :].astype(F32) < counts, 0.0, NEG)
        bias[pl.ds(first, count), :TILES] = near
        bias[pl.ds(first, count), TILES:] = near

    set_bias(0, SIDES, cnt)

    @pl.loop(0, PAIRS)
    def _(p):
        queries = both(q_ref[:, lanes(p)])
        scores = dot(kall[pl.ds(0, SIDES), lanes(p)], queries, ((1,), (1,))) * HEAD_SCALE + bias[:SIDES, :]
        highest = jnp.max(scores, axis=0, keepdims=True)
        raised = jnp.exp(scores - highest)
        prob[p, :SIDES, :] = raised
        peak[p] = jnp.broadcast_to(highest, (8, 2 * TILES))
        mass[p] = jnp.broadcast_to(jnp.sum(raised, axis=0, keepdims=True), (8, 2 * TILES))

    for copy in first:
        copy.arrived()
    corn[...] = dot(corners_ref[...], held[pl.ds(0, 96), :]).astype(BF)
    second = [
        send(corn.at[pl.ds(0, 48)], held.at[pl.ds(144, 48)], up, **to_up),
        send(corn.at[pl.ds(48, 48)], held.at[pl.ds(96, 48)], down, **to_down),
        send(beside.at[1], beside.at[2], up, **to_up),
        send(beside.at[1], beside.at[0], down, **to_down),
    ]

    gathers = []
    for step, offset, size in plan:
        own_at = pl.multiple_of(core * half + offset, 16)
        at = pl.multiple_of(dp * part + core * half + offset, 16)
        gathers.append(
            send(w_ref.at[pl.ds(own_at, size)], wfull.at[pl.ds(at, size)], along_z(step))
        )

    for copy in second:
        copy.arrived()
    side_keys = dot(sides_ref[...], held[...])
    kall[pl.ds(SIDES, 96), :] = side_keys[:96].astype(BF)
    vall[pl.ds(SIDES, 96), :] = side_keys[96:].astype(BF)
    set_bias(SIDES, KEYS - SIDES, beside)

    def forward(p):
        keys, values = kall[pl.ds(SIDES, KEYS - SIDES), lanes(p)], vall[:, lanes(p)]
        scores = dot(keys, both(q_ref[:, lanes(p)]), ((1,), (1,))) * HEAD_SCALE + bias[SIDES:, :]
        before = peak[p][:1]
        highest = jnp.maximum(before, jnp.max(scores, axis=0, keepdims=True))
        raised = jnp.exp(scores - highest)
        scale = jnp.exp(before - highest)
        inverse = 1.0 / (scale * mass[p][:1] + jnp.sum(raised, axis=0, keepdims=True))
        weights = jnp.concatenate([prob[p, :SIDES, :] * (scale * inverse), raised * inverse], axis=0)
        prob[p] = weights
        mixed = own_heads(dot(values, weights.astype(BF), ((0,), (0,))))
        attn_t[pl.ds(pl.multiple_of(p * PAIR, PAIR), PAIR), :] = (mixed * valid_lane).astype(BF)

    strip_rows = part // Y

    def term_of(h, which):
        columns = pl.ds(pl.multiple_of(which * 384, 128), 384)
        return dot(attn_t[pl.ds(384 * h, 384), :], go_ref[:, columns])

    def cut(term, i, j):
        return term[i * part + j * strip_rows :][:strip_rows]

    core_copies = []
    for h in range(2):
        pl.loop(3 * h, 3 * h + 3)(forward)
        term = term_of(h, 1 - core)
        for j in range(Y):
            for i in range(2):
                core_out[h, j, i] = cut(term, i, j).astype(BF)
        core_copies.append(send(core_out.at[h], core_in.at[h], partner))
        term = term_of(h, core)
        for j in range(Y):
            for i in range(2):
                gw_own[h, j, i] = cut(term, i, j)

    y_copies, x_copies = [], []
    for h in range(2):
        core_copies[h].arrived()
        for j in range(Y):
            for i in range(2):
                d = 2 * h + i
                total = gw_own[h, j, i] + core_in[h, j, i].astype(F32)
                xy_sum[j, d] = total
                if (d + j) % 2 == 0:
                    y_out[h, j] = total.astype(BF)
                else:
                    x_out[d, j // 2] = total.astype(BF)
        for s in range(1, Y):
            y_copies.append(send(y_out.at[h, (y + s) % Y], y_in.at[s - 1, h], along_y(s)))
        for s in range(1, X):
            there = (x + s) % X
            x_copies.append(
                send(x_out.at[there], x_in.at[s - 1], along_x(s), sends=there // 2 == h, gets=x // 2 == h)
            )

    passed = []
    for copy, (step, offset, size) in zip(gathers, plan):
        copy.arrived()
        source = (dp - step + DP) % DP
        at = pl.multiple_of(source * part + core * half + offset, 16)
        there = wfull.at[pl.ds(at, size)]
        passed.append(send(there, there, partner))
    pl.semaphore_signal(far, inc=1, device_id=along_hi(1), device_id_type=MESH)
    for copy in passed:
        copy.arrived()
    back = dot(go_ref[...], wfull[...], ((1,), (1,))).astype(BF)
    gated[...] = back * valid_row.astype(BF)

    def backward(p):
        keys, values = kall[:, lanes(p)], vall[:, lanes(p)]
        queries, grads = both(q_ref[:, lanes(p)]), both(gated[:, lanes(p)])
        weights = prob[p]
        prob_grad = dot(values, grads, ((1,), (1,)))
        correction = jnp.sum(weights * prob_grad, axis=0, keepdims=True)
        score_grad = (weights * (prob_grad - correction) * HEAD_SCALE).astype(BF)
        key_part = dot(score_grad, queries)
        value_part = dot(weights.astype(BF), grads)
        dk_own[:, lanes(p)] = key_part[:TILES]
        dv_own[:, lanes(p)] = value_part[:TILES]
        row_out[0, :, lanes(p)] = key_part[UP:DOWN].astype(BF)
        row_out[1, :, lanes(p)] = value_part[UP:DOWN].astype(BF)
        row_out[2, :, lanes(p)] = key_part[DOWN:SIDES].astype(BF)
        row_out[3, :, lanes(p)] = value_part[DOWN:SIDES].astype(BF)
        dcol[pl.ds(0, 96), lanes(p)] = key_part[SIDES:].astype(BF)
        dcol[pl.ds(96, 96), lanes(p)] = value_part[SIDES:].astype(BF)
        query_part = own_heads(dot(keys, score_grad, ((0,), (0,))))
        dq_ref[:, lanes(p)] = query_part.T.astype(BF)

    def run(first, last):
        if UNROLLED:
            for p in range(first, last):
                backward(p)
        else:
            pl.loop(first, last)(backward)

    run(0, 2)
    for copy in y_copies + x_copies:
        copy.arrived()
    for i in range(2):
        total = xy_sum[y, 2 * i + y % 2]
        for s in range(1, Y):
            total = total + y_in[s - 1, i].astype(F32)
        half_sum[i] = total
        half_out[i] = total.astype(BF)
        total = xy_sum[2 * i + (x + 1) % 2, x]
        for s in range(1, X):
            total = total + x_in[s - 1, i].astype(F32)
        half_sum[2 + i] = total
        half_out[2 + i] = total.astype(BF)
    odd = (x + y) % 2
    second_copies = []
    for s in range(1, X):
        there = (x + s) % X
        second_copies.append(
            send(half_out.at[there // 2], e_in.at[s - 1], along_x(s), sends=(there + y) % 2 == 0, gets=odd == 0)
        )
    for s in range(1, Y):
        there = (y + s) % Y
        second_copies.append(
            send(half_out.at[2 + there // 2], e_in.at[s - 1], along_y(s), sends=(there + x) % 2 == 1, gets=odd == 1)
        )

    run(2, 5)
    for copy in second_copies:
        copy.arrived()
    total = half_sum[odd * (2 + y // 2) + (1 - odd) * (x // 2)]
    for s in range(1, X):
        total = total + e_in[s - 1].astype(F32)
    z_out[...] = total.astype(BF)
    keeper = dp == x
    behind = (z + Z - x) % DP
    z_copies = [
        send(z_out, z_in.at[i], along_z(step), sends=behind == (DP - step) % DP, gets=keeper)
        for i, step in enumerate((-1, 1, -2))
    ]

    run(5, 6)
    bcorn[...] = dot(bcorn_ref[...], dcol[...]).astype(BF)
    back_corners = [
        send(bcorn.at[pl.ds(0, 48)], bcorn_in.at[pl.ds(48, 48)], up, **to_up),
        send(bcorn.at[pl.ds(48, 48)], bcorn_in.at[pl.ds(0, 48)], down, **to_down),
    ]
    back_rows = [
        send(row_out.at[pl.ds(0, 2)], row_in.at[pl.ds(2, 2)], up, **to_up),
        send(row_out.at[pl.ds(2, 2)], row_in.at[pl.ds(0, 2)], down, **to_down),
    ]

    for copy in z_copies:
        copy.arrived()

    @pl.when(keeper)
    def _():
        gathered = total
        for s in range(1, DP):
            gathered = gathered + z_in[s - 1].astype(F32)
        h_all[zh] = gathered.astype(BF)

    pl.semaphore_wait(far, 1)
    h_copies = [
        send(h_all.at[zh], h_all.at[zh], along_hi(s), sends=keeper, gets=keeper)
        for s in range(1, ZH)
    ]
    for copy in back_corners:
        copy.arrived()
    returned = dot(bstrip_ref[:, :192], dcol[...]) + dot(bstrip_ref[:, 192:], bcorn_in[...])
    bstrip[...] = returned.astype(BF)
    back_strips = [
        send(bstrip.at[pl.ds(0, 48)], bstrip_in.at[pl.ds(48, 48)], left, **to_left),
        send(bstrip.at[pl.ds(48, 48)], bstrip_in.at[pl.ds(0, 48)], right, **to_right),
    ]

    for copy in h_copies:
        copy.arrived()

    @pl.when(keeper)
    def _():
        final = h_all[0].astype(F32)
        for s in range(1, ZH):
            final = final + h_all[s].astype(F32)
        g_all[core, y] = final.astype(BF)

    own_piece = g_all.at[core, y]
    spread = [
        send(own_piece, own_piece, along_x(s), sends=keeper, gets=(x + X - s) % X == dp)
        for s in range(1, X)
    ]
    for copy in back_rows:
        copy.arrived()
    for kind, total in enumerate((dk_own, dv_own)):
        total[pl.ds(0, 48), :] += row_in[kind].astype(F32)
        total[pl.ds(80, 48), :] += row_in[2 + kind].astype(F32)

    for copy in spread:
        copy.arrived()
    spread_y = [send(own_piece, own_piece, along_y(s)) for s in range(1, Y)]
    core_back = [send(own_piece, own_piece, partner)]

    for copy in back_strips:
        copy.arrived()
    edge = bstrip_in[...]
    for kind, (total, out) in enumerate(((dk_own, dk_ref), (dv_own, dv_ref))):
        side_term = dot(unpack_ref[pl.ds(TILES * kind, TILES), :], edge)
        out[...] = (total[...] + side_term).astype(BF)

    for s, copy in zip(range(1, Y), spread_y):
        copy.arrived()
        piece = g_all.at[core, (y + Y - s) % Y]
        core_back.append(send(piece, piece, partner))
    for copy in core_back:
        copy.arrived()
    norm = (TILES * DP * ROWS * COLS) ** (-0.5)
    for c in range(2):
        for j in range(Y):
            gw_ref[pl.ds(j * strip_rows, strip_rows), pl.ds(c * 384, 384)] = (
                g_all[c, j].astype(F32) * norm
            )
    for copy in started:
        copy.sent()


COPIES = 72
UNROLLED = False
LIMIT = 67043328


def deliver(*refs):
    sources, targets, held, into, out = refs[:4], refs[4:8], refs[8:12], refs[12], refs[13]
    first = [pltpu.make_async_copy(s, h, into.at[i]) for i, (s, h) in enumerate(zip(sources, held))]
    then = [pltpu.make_async_copy(h, t, out.at[i]) for i, (h, t) in enumerate(zip(held, targets))]
    for copy in first:
        copy.start()
    for copy, following in zip(first, then):
        copy.wait()
        following.start()
    for copy in then:
        copy.wait()


def on_device(sizes, queries, keys, values, occupancy, out_weight, grad_out):
    DP, ROWS, COLS, X = sizes
    Y, ZH = ROWS // 2, COLS // X
    part = CH // DP
    strip_rows = part // Y
    flat = [a.reshape(TILES, CH) for a in (queries, keys, values, grad_out)]
    vmem = pl.BlockSpec(memory_space=pltpu.VMEM)
    hbm = pl.BlockSpec(memory_space=pltpu.HBM)
    fixed = tables()
    piece = (strip_rows, 384)
    scratch = [
        pltpu.VMEM((TILES, CH), BF),
        pltpu.VMEM((TILES, CH), BF),
        pltpu.VMEM((part, CH), BF),
        pltpu.SMEM((1, 2), jnp.int32),
        *(pltpu.VMEM(t.shape, BF) for t in fixed),
        pltpu.VMEM((KEYS, CH), BF),
        pltpu.VMEM((KEYS, CH), BF),
        pltpu.VMEM((96, CH), BF),
        pltpu.VMEM((192, CH), BF),
        pltpu.VMEM((96, CH), BF),
        pltpu.VMEM((3, 2, 8, 128), F32),
        pltpu.VMEM((3, 2, 8, 128), F32),
        pltpu.VMEM((CH, CH), BF),
        pltpu.VMEM((KEYS, 2 * TILES), F32),
        pltpu.VMEM((PAIRS, KEYS, 2 * TILES), F32),
        pltpu.VMEM((PAIRS, 8, 2 * TILES), F32),
        pltpu.VMEM((PAIRS, 8, 2 * TILES), F32),
        pltpu.VMEM((CH, TILES), BF),
        pltpu.VMEM((TILES, CH), BF),
        pltpu.VMEM((TILES, CH), F32),
        pltpu.VMEM((TILES, CH), F32),
        pltpu.VMEM((4, 48, CH), BF),
        pltpu.VMEM((4, 48, CH), BF),
        pltpu.VMEM((192, CH), BF),
        pltpu.VMEM((96, CH), BF),
        pltpu.VMEM((96, CH), BF),
        pltpu.VMEM((96, CH), BF),
        pltpu.VMEM((96, CH), BF),
        pltpu.VMEM((2, Y, 2) + piece, F32),
        pltpu.VMEM((2, Y, 2) + piece, BF),
        pltpu.VMEM((2, Y, 2) + piece, BF),
        pltpu.VMEM((Y, DP) + piece, F32),
        pltpu.VMEM((2, Y) + piece, BF),
        pltpu.VMEM((Y - 1, DP // 2) + piece, BF),
        pltpu.VMEM((DP, Y // 2) + piece, BF),
        pltpu.VMEM((X - 1, Y // 2) + piece, BF),
        pltpu.VMEM((4,) + piece, F32),
        pltpu.VMEM((4,) + piece, BF),
        pltpu.VMEM((3,) + piece, BF),
        pltpu.VMEM(piece, BF),
        pltpu.VMEM((DP - 1,) + piece, BF),
        pltpu.VMEM((ZH,) + piece, BF),
        pltpu.VMEM((2, Y) + piece, BF),
        pltpu.SemaphoreType.DMA((COPIES,)),
        pltpu.SemaphoreType.DMA((COPIES,)),
        pltpu.SemaphoreType.DMA((14,)),
        pltpu.SemaphoreType.REGULAR,
    ]
    tile_out = jax.ShapeDtypeStruct((TILES, CH), BF)
    outs = (tile_out, tile_out, tile_out, jax.ShapeDtypeStruct((part, CH), F32))
    made = pl.pallas_call(
        functools.partial(body, sizes),
        out_shape=outs,
        in_specs=[hbm] * 14,
        out_specs=(vmem,) * 4,
        scratch_shapes=scratch,
        compiler_params=pltpu.CompilerParams(
            collective_id=0, has_side_effects=True, vmem_limit_bytes=LIMIT
        ),
        name="neighbourhood",
    )(*flat, out_weight, occupancy.reshape(1, 2), *(jnp.asarray(t) for t in fixed))
    grad_q, grad_k, grad_v, grad_w = pl.pallas_call(
        deliver,
        out_shape=outs,
        in_specs=[hbm] * 4,
        out_specs=(hbm,) * 4,
        scratch_shapes=[pltpu.VMEM(o.shape, o.dtype) for o in outs]
        + [pltpu.SemaphoreType.DMA((4,)), pltpu.SemaphoreType.DMA((4,))],
        compiler_params=pltpu.CompilerParams(vmem_limit_bytes=LIMIT),
        name="deliver",
    )(*made)
    shape = (1, HIGH, WIDE, CH)
    return grad_q.reshape(shape), grad_k.reshape(shape), grad_v.reshape(shape), grad_w


def solution(mesh):
    dp = mesh.shape["dp"]
    sizes = (dp, mesh.shape["row"], mesh.shape["col"], dp)
    tiles = P("dp", "row", "col", None)
    return jax.shard_map(
        functools.partial(on_device, sizes),
        mesh=mesh,
        in_specs=(tiles, tiles, tiles, P("dp", "row", "col"), P("dp", None), tiles),
        out_specs=(tiles, tiles, tiles, P("dp", None)),
        check_vma=False,
    )
```
